32 devices in a mesh: sub: 16 (over z, y, core), strip: 2 (over x).
Axes of the slice: x: 2, y: 2, z: 4, core: 2. Of those that a mesh axis runs over, the one named last changes fastest.
Arguments:
- spectra: bfloat16 [32, 256, 2048], P('sub', 'strip'), may hold values from -6 to 6
- offsets: int32 [32], P('sub'), may hold values from 0 to 1023
Outputs:
- foreground: float32 [1024, 256, 32], P('strip', 'sub')
The draws below stay inside these ranges and needn't reach their ends.
All inputs are finite; a program needn't handle non-finite values.
Results may differ from the reference program's by a relative error of at most 0.0068.
Values may be sent and summed in bfloat16 or wider, within the bound.
A program may use at most 64 MiB of HBM per device.

```python
import math
import jax
import jax.numpy as jnp
from jax import lax

KR = 256
KA = 1024
ROWS = 1024
COLS = 256
WIN = 8
BG = 16
SUBAP = 32


def set_ends(entries, own_key, smallest, largest):
    longest = entries.shape.index(max(entries.shape))
    spots = []
    for shift in (0, 1):
        where = [jax.random.randint(jax.random.fold_in(own_key, axis), (), 0, length) for axis, length in enumerate(entries.shape)]
        where[longest] = (where[longest] + shift) % entries.shape[longest]
        spots.append(tuple(where))
    return entries.at[spots[0]].set(smallest).at[spots[1]].set(largest)


def steps_of(key, shape, pieces, low, largest):
    level, own = 1.0, jax.random.fold_in(key, 6)
    for axis_at, blocks in pieces:
        draws = jnp.exp(jax.random.uniform(jax.random.fold_in(own, axis_at), (blocks,), jnp.float32, low / len(pieces), largest / len(pieces)))
        level = level * jnp.repeat(draws, shape[axis_at] // blocks).reshape([-1 if axis == axis_at else 1 for axis in range(len(shape))])
    return level


def gaussian(stream_key, dims, scale, bound, cuts=(), held_as=jnp.bfloat16):
    result = jax.random.normal(stream_key, dims, jnp.float32) * scale
    if len(cuts) > 0:
        result = steps_of(stream_key, dims, cuts, -0.22, 0.18) * result
    return jnp.clip(result, min=-bound, max=bound).astype(held_as)


def setup_inputs(seed: int = 0) -> dict:
    keys = jax.random.split(jax.random.key(seed), 3)
    return {
        "spectra": gaussian(keys[0], (SUBAP, KR, 2 * KA), 1.0, 6.0, ((0, 16), (1, 2))),
        "offsets": set_ends(jax.random.randint(keys[1], (SUBAP,), 0, ROWS), jax.random.fold_in(keys[1], 1), 0, ROWS - 1).astype(jnp.int32),
    }


def column_table(samples, width):
    sample_index = jnp.arange(samples, dtype=jnp.int32)[:, None]
    column_index = jnp.arange(width, dtype=jnp.int32)[None, :]
    phase = jnp.mod(sample_index * column_index, samples).astype(jnp.float32) * (2.0 * math.pi / samples)
    cosine = jnp.cos(phase) / math.sqrt(samples)
    sine = -jnp.sin(phase) / math.sqrt(samples)
    upper = jnp.concatenate([cosine, sine], axis=1)
    lower = jnp.concatenate([-sine, cosine], axis=1)
    return jnp.concatenate([upper, lower], axis=0).astype(jnp.bfloat16)

def row_table(row_index, samples, image_rows):
    sample_index = jnp.arange(samples, dtype=jnp.int32)[None, :] - samples // 2
    phase = jnp.mod(row_index[:, None] * sample_index, image_rows).astype(jnp.float32) * (2.0 * math.pi / image_rows)
    scale = 1.0 / math.sqrt(samples)
    return jnp.concatenate([jnp.cos(phase) * scale, jnp.sin(phase) * scale], axis=0).astype(jnp.bfloat16)

def apply_phase(mixed, offset, sample_index, samples, image_rows, width):
    angle = jnp.mod(offset * (sample_index - samples // 2), image_rows).astype(jnp.float32) * (2.0 * math.pi / image_rows)
    cosine = jnp.cos(angle)[:, None]
    sine = jnp.sin(angle)[:, None]
    real_part = mixed[:, :width]
    imag_part = mixed[:, width:]
    return jnp.concatenate([real_part * cosine - imag_part * sine, real_part * sine + imag_part * cosine], axis=1).astype(jnp.bfloat16)

def reference(spectra, offsets):
    columns = column_table(KA, COLS)
    table = row_table(jnp.arange(ROWS, dtype=jnp.int32), KR, ROWS)
    samples_all = jnp.arange(KR, dtype=jnp.int32)

    def single(inputs):
        spectrum, offset = inputs
        mixed = jnp.dot(spectrum, columns, preferred_element_type=jnp.float32)
        shifted = apply_phase(mixed, offset, samples_all, KR, ROWS, COLS)
        product = jnp.dot(table, shifted, preferred_element_type=jnp.float32)
        real_part = product[:ROWS, :COLS] - product[ROWS:, COLS:]
        imag_part = product[:ROWS, COLS:] + product[ROWS:, :COLS]
        return jnp.concatenate([real_part, imag_part], axis=1)
    images = lax.map(single, (spectra, offsets))
    frames = images
    for lead in range(1, WIN):
        frames = frames + jnp.roll(images, -lead, axis=0)
    real_part = frames[:, :, :COLS]
    imag_part = frames[:, :, COLS:]
    log_power = jnp.log(1.0 + real_part * real_part + imag_part * imag_part)
    padded = jnp.pad(log_power, ((0, 0), (1, 1), (1, 1)))
    total = jnp.zeros_like(log_power)
    for row_step in range(3):
        for col_step in range(3):
            total = total + padded[:, row_step:row_step + ROWS, col_step:col_step + COLS]
    filtered = total / 9.0
    background = jnp.zeros_like(filtered)
    for behind in range(BG):
        background = background + jnp.roll(filtered, behind, axis=0)
    background = background / BG
    return jnp.transpose(filtered - background, (1, 2, 0))
```

```python
import functools
import math

import jax
import jax.numpy as jnp
import numpy as np
from jax import lax
from jax.experimental import pallas as pl
from jax.experimental.pallas import tpu as pltpu
from jax.sharding import PartitionSpec as P

KR = 256
ROWS = 1024
COLS = 256
WIN = 8
BG = 16


def column_table(samples, parts):
    wide = COLS // parts + 2
    column = (np.arange(parts) * (wide - 2))[:, None] + np.arange(-1, wide - 1)[None, :]
    inside = (column >= 0) & (column < COLS)
    phase = ((np.arange(samples)[:, None, None] * column[None]) % samples) * (2.0 * math.pi / samples)
    cosine = np.where(inside, np.cos(phase), 0.0) / math.sqrt(samples)
    sine = np.where(inside, -np.sin(phase), 0.0) / math.sqrt(samples)
    upper = np.stack([cosine, sine], axis=2)
    lower = np.stack([-sine, cosine], axis=2)
    return jnp.asarray(np.concatenate([upper, lower], axis=0).astype(np.float32)).astype(jnp.bfloat16)


def row_table(rows):
    sample = jnp.arange(KR, dtype=jnp.int32)[:, None] - KR // 2
    phase = jnp.mod(rows[None, :] * sample, ROWS).astype(jnp.float32) * (2.0 * math.pi / ROWS)
    scale = jnp.where((rows >= 0) & (rows < ROWS), 1.0 / math.sqrt(KR), 0.0)[None, :]
    cosine = jnp.cos(phase) * scale
    sine = jnp.sin(phase) * scale
    upper = jnp.stack([cosine, sine], axis=1)
    lower = jnp.stack([-sine, cosine], axis=1)
    return jnp.concatenate([upper, lower], axis=0).astype(jnp.bfloat16)


def rotation(offsets, samples):
    angle = jnp.mod(offsets[:, None] * (samples[None, :] - KR // 2), ROWS).astype(jnp.float32) * (2.0 * math.pi / ROWS)
    return jnp.cos(angle), jnp.sin(angle)


def plain_body(spectra, offsets):
    own, depth = spectra.shape[:2]
    parts, strips = lax.axis_size("sub"), lax.axis_size("strip")
    wide = COLS // parts + 2
    high = ROWS // strips
    strip = lax.axis_index("strip")
    frames = own * parts
    table = column_table(spectra.shape[2] // 2, parts)
    cosine, sine = rotation(offsets, strip * depth + jnp.arange(depth, dtype=jnp.int32))
    mixed = jnp.einsum("skc,cdpn->dspnk", spectra, table, preferred_element_type=jnp.float32)
    real, imag = mixed[:, :, 0], mixed[:, :, 1]
    cosine, sine = cosine[None, :, None, :], sine[None, :, None, :]
    shifted = jnp.stack([real * cosine - imag * sine, real * sine + imag * cosine], axis=2).astype(jnp.bfloat16)
    held = lax.all_to_all(shifted, "sub", split_axis=0, concat_axis=0, tiled=True)
    held = held.reshape(frames, 2, wide, depth)
    whole = jnp.zeros((frames, 2, wide, strips, depth), jnp.bfloat16)
    for step in range(strips):
        part = held
        if step:
            part = lax.ppermute(held, "strip", [(i, (i + step) % strips) for i in range(strips)])
        source = jnp.mod(strip - step, strips)
        whole = lax.dynamic_update_slice(whole, part[:, :, :, None], (0, 0, 0, source, 0))
    wider = whole.reshape(frames, 2, wide, KR).astype(jnp.float32)
    summed = wider
    for lead in range(1, WIN):
        summed = summed + jnp.roll(wider, -lead, axis=0)
    rows = strip * high + jnp.arange(-1, high + 1, dtype=jnp.int32)
    product = jnp.einsum(
        "fpnk,pkqm->qnfm",
        summed.astype(jnp.bfloat16),
        row_table(rows).reshape(2, KR, 2, high + 2),
        preferred_element_type=jnp.float32,
    )
    log_power = jnp.log(1.0 + product[0] * product[0] + product[1] * product[1])
    total = log_power[:, :, :-2] + log_power[:, :, 1:-1] + log_power[:, :, 2:]
    filtered = (total[:-2] + total[1:-1] + total[2:]) / 9.0
    background = filtered
    for behind in range(1, BG):
        background = background + jnp.roll(filtered, behind, axis=1)
    return jnp.transpose(filtered - background / BG, (2, 0, 1))


LANES = 128
GROUP = 4
MESH = pl.DeviceIdType.MESH


def column_planes(samples):
    phase = (np.arange(COLS)[:, None] * np.arange(samples)[None, :] % samples) * (2.0 * math.pi / samples)
    planes = np.stack([np.cos(phase), -np.sin(phase)]) / math.sqrt(samples)
    return jnp.asarray(planes.astype(np.float32).astype(jnp.bfloat16))


def row_planes(high):
    row = np.concatenate([np.arange(high + LANES - 1), [-1]])
    used = (row <= high)[None, :]
    sample = np.arange(KR)[:, None] - KR // 2
    phase = (row[None, :] * sample % ROWS) * (2.0 * math.pi / ROWS)
    planes = np.stack([np.cos(phase) * used, np.sin(phase) * used]) / math.sqrt(KR)
    return jnp.asarray(planes.astype(np.float32).astype(jnp.bfloat16))


def frame_weights(width, sources, rows):
    frames = 2 * sources
    weights = np.zeros((width, frames, rows), np.float32)
    target = np.arange(frames)

    def place(at, column, frame):
        series = np.where(target == frame, 1.0, 0.0) - np.where((target - frame) % frames < BG, 1.0 / BG, 0.0)
        for near in range(max(column - 1, 0), min(column + 2, width)):
            weights[near, :, at] = series

    for lane in range(2):
        for source in range(sources):
            frame = 2 * source + lane
            for column in range(width):
                place((lane * sources + source) * width + column, column, frame)
            for side in range(2):
                place(2 * sources * width + (lane * sources + source) * 2 + side, (-1, width)[side], frame)
    return jnp.asarray(weights.reshape(width * frames, rows).astype(jnp.bfloat16))


def product_of(a, b):
    return lax.dot_general(a, b, (((1,), (0,)), ((), ())), preferred_element_type=jnp.float32)


def product_t(a, b):
    return lax.dot_general(a, b, (((1,), (1,)), ((), ())), preferred_element_type=jnp.float32)


def ahead(value, steps):
    return jnp.concatenate([value[steps:], value[:steps]], axis=0)


def kernel(
    parts, strips, offsets_hbm, spectra_hbm, columns_hbm, rows_hbm, weights_hbm, out_ref,
    offsets_ref, spectra, columns, rows, weights, real, imag, edge, main, held, lhs, boxed, level,
    load_sem, own_sem, send_sem, recv_sem, pass_sem, got_sem,
):
    me, strip = lax.axis_index("sub"), lax.axis_index("strip")
    width = COLS // parts
    depth = spectra.shape[1]
    samples = spectra.shape[2] // 2
    high = out_ref.shape[2]
    other = 1 - strip
    layers = parts // GROUP
    reach = layers // 2
    layer, place = me // GROUP, lax.rem(me, GROUP)
    upper, within = layer // reach, lax.rem(layer, reach)

    def device_at(half, step, turn):
        return (half * reach + step) * GROUP + lax.rem(place + turn + GROUP, GROUP)

    close = [device_at(upper, within, turn) for turn in range(1, GROUP)]
    close += [
        device_at(upper, lax.rem(within + step, reach), turn) for step in range(1, reach) for turn in range(GROUP)
    ]
    outward = [(1 - upper) * (reach - 1) + (2 * upper - 1) * step for step in range(reach)]
    targets = [device_at(1 - upper, step, turn) for step in outward for turn in range(GROUP)]
    origins = [device_at(1 - upper, step, -turn) for step in outward for turn in range(GROUP)]

    loads = [
        pltpu.make_async_copy(source, target, load_sem.at[i])
        for i, (source, target) in enumerate(
            [(offsets_hbm, offsets_ref), (spectra_hbm, spectra), (columns_hbm, columns), (rows_hbm, rows), (weights_hbm, weights)]
        )
    ]
    for load in loads[:3]:
        load.start()
    barrier = pltpu.get_barrier_semaphore()
    for away in range(1, parts):
        pl.semaphore_signal(barrier, inc=1, device_id=(lax.rem(me + away, parts), strip), device_id_type=MESH)
    for near in [me] + close:
        pl.semaphore_signal(barrier, inc=1, device_id=(near, other), device_id_type=MESH)

    loads[0].wait()
    lane = lax.broadcasted_iota(jnp.int32, (1, 2 * depth), 1)
    sample = strip * depth + jnp.where(lane < depth, lane, lane - depth) - KR // 2
    offset = jnp.where(lane < depth, offsets_ref[0], offsets_ref[1])
    angle = jnp.bitwise_and(offset * sample, ROWS - 1).astype(jnp.float32) * (2.0 * math.pi / ROWS)
    cosine, sine = jnp.cos(angle), jnp.sin(angle)
    edge[...] = jnp.zeros_like(edge)
    loads[1].wait()
    loads[2].wait()
    for load in loads[3:]:
        load.start()
    data = spectra[...].reshape(2 * depth, 2 * samples)
    data_re, data_im = data[:, :samples], data[:, samples:]
    step = COLS
    for at in range(0, COLS, step):
        cos_part, sin_part = columns[0, at : at + step], columns[1, at : at + step]
        re = product_t(cos_part, data_re) - product_t(sin_part, data_im)
        im = product_t(sin_part, data_re) + product_t(cos_part, data_im)
        first = at // width
        for part, value, ref in ((0, re * cosine - im * sine, real), (1, re * sine + im * cosine, imag)):
            ref[at : at + step] = value
            blocks = value.reshape(step // width, width // 4, 4, 2 * depth).astype(jnp.bfloat16)
            for own in range(2):
                main[
                    first : first + step // width, own * width // 4 : (own + 1) * width // 4, :, part * depth : (part + 1) * depth
                ] = blocks[:, :, :, own * depth : (own + 1) * depth]
    for part, ref in ((0, real), (1, imag)):
        for own in range(2):
            lanes, into = slice(own * depth, (own + 1) * depth), slice(part * depth, (part + 1) * depth)
            for d in range(parts):
                if d > 0:
                    edge[d, 2 * own : 2 * own + 1, into] = ref[d * width - 1 : d * width, lanes]
                if d < parts - 1:
                    edge[d, 2 * own + 1 : 2 * own + 2, into] = ref[(d + 1) * width : (d + 1) * width + 1, lanes]
    main[:, 2 * width // 4] = edge[:, :4].astype(jnp.bfloat16)

    pl.semaphore_wait(barrier, parts + len(close))

    def send(to):
        return pltpu.make_async_remote_copy(
            src_ref=main.at[to], dst_ref=held.at[strip, me], send_sem=send_sem.at[to],
            recv_sem=recv_sem.at[me], device_id=(to, strip), device_id_type=MESH,
        )

    def arrival(h, source, sem):
        return pltpu.make_async_remote_copy(
            src_ref=main.at[source], dst_ref=held.at[h, source], send_sem=send_sem.at[source],
            recv_sem=sem.at[source], device_id=(source, strip), device_id_type=MESH,
        )

    def cross(to):
        return pltpu.make_async_remote_copy(
            src_ref=main.at[to], dst_ref=held.at[strip, me], send_sem=pass_sem.at[to],
            recv_sem=got_sem.at[me], device_id=(to, other), device_id_type=MESH,
        )

    def forward(source):
        return pltpu.make_async_remote_copy(
            src_ref=held.at[strip, source], dst_ref=held.at[strip, source], send_sem=pass_sem.at[source],
            recv_sem=got_sem.at[source], device_id=(me, other), device_id_type=MESH,
        )

    for to, near in zip(targets, [me] + close):
        send(to).start()
        cross(near).start()
    for to in close:
        send(to).start()
    kept = pltpu.make_async_copy(main.at[me], held.at[strip, me], own_sem.at[0])
    kept.start()
    for source in origins:
        arrival(strip, source, recv_sem).wait_recv()
        forward(source).start()
    for source in close:
        arrival(strip, source, recv_sem).wait_recv()
    top = 2 * parts * width
    odd = lax.rem(lax.broadcasted_iota(jnp.int32, (1, 1, 2 * depth), 2), 2)
    sign = 1.0 - 2.0 * (odd * strip).astype(jnp.float32)
    row_at = lax.broadcasted_iota(jnp.int32, (parts, 8, 2 * depth), 1)
    def window(h):
        whole = held[h].astype(jnp.float32) * sign[None]
        block = whole[:, : 2 * width // 4].reshape(parts, 2 * width, 2 * depth)
        first, second = block[:, :width], block[:, width:]
        near = whole[:, 2 * width // 4]
        near = jnp.concatenate([near, jnp.zeros_like(near)], axis=1)
        near_second = jnp.concatenate([pltpu.roll(near[i], 6, 0)[None] for i in range(parts)], axis=0)
        for is_halo, one, two in ((False, first, second), (True, near, near_second)):
            pair = one + two
            double = pair + ahead(pair, 1)
            quad = double + ahead(double, 2)
            for own, frame in ((0, quad), (1, quad - one + ahead(one, WIN // 2))):
                if is_halo:
                    frame = jnp.where(row_at < 2, frame, 0.0)
                    packed = []
                    for group in range(parts // 4):
                        total = frame[4 * group]
                        for j in range(1, 4):
                            total = total + pltpu.roll(frame[4 * group + j], 2 * j, 0)
                        packed.append(total)
                    flat = jnp.concatenate(packed, axis=0).astype(jnp.bfloat16)
                    at, size = top + own * 2 * parts, 2 * parts
                else:
                    flat = frame.reshape(parts * width, 2 * depth).astype(jnp.bfloat16)
                    at, size = own * parts * width, parts * width
                for part in range(2):
                    lhs[at : at + size, pl.ds(pl.multiple_of(part * KR + h * depth, depth), depth)] = flat[
                        :, part * depth : (part + 1) * depth
                    ]

    kept.wait()
    window(strip)
    for source in [me] + close + origins:
        arrival(other, source, got_sem).wait_recv()
    window(other)
    loads[3].wait()
    total_rows = top + 4 * parts
    tail = lax.broadcasted_iota(jnp.int32, (1, high + LANES), 1)
    outside = ((tail == high) & (strip == strips - 1)) | ((tail == high + LANES - 1) & (strip == 0))
    inside = jnp.where(outside, 0.0, 1.0)
    chunk = total_rows // 3
    for at in range(0, total_rows, chunk):
        left_re, left_im = lhs[at : at + chunk, :KR], lhs[at : at + chunk, KR:]
        re = product_of(left_re, rows[0]) - product_of(left_im, rows[1])
        im = product_of(left_re, rows[1]) + product_of(left_im, rows[0])
        power = jnp.log(1.0 + re * re + im * im) * inside
        summed = power + pltpu.roll(power, 1, 1) + pltpu.roll(power, high + LANES - 1, 1)
        boxed[at : at + chunk] = summed[:, :high]

    frames = 2 * parts
    block = boxed[:top].reshape(frames, width, high)
    mean = jnp.sum(block, axis=0, keepdims=True) * (1.0 / frames)
    level[:top] = (block - mean).reshape(top, high).astype(jnp.bfloat16)
    near = boxed[top:total_rows].reshape(frames // 4, 8, high)
    mean = jnp.sum(near, axis=0) * (1.0 / frames)
    mean = mean + pltpu.roll(mean, 4, 0)
    mean = mean + pltpu.roll(mean, 2, 0)
    level[top:total_rows] = (near - mean[None]).reshape(total_rows - top, high).astype(jnp.bfloat16)
    level[total_rows:] = jnp.zeros((level.shape[0] - total_rows, high), jnp.bfloat16)
    loads[4].wait()
    for c in range(0, width, 4):
        piece = product_of(weights[c * frames : (c + 4) * frames], level[...])
        out_ref[c : c + 4] = (piece * (1.0 / 9.0)).reshape(4, frames, high)
    for to in targets + close:
        send(to).wait_send()
    for to in [me] + close:
        cross(to).wait_send()
    for source in origins:
        forward(source).wait_send()


def kernel_body(spectra, offsets):
    parts, strips = lax.axis_size("sub"), lax.axis_size("strip")
    own, depth, both = spectra.shape
    width, high = COLS // parts, ROWS // strips
    frames = own * parts
    total_rows = frames * (width + 2)
    padded = -(-total_rows // LANES) * LANES
    bf16, f32 = jnp.bfloat16, jnp.float32
    operands = (offsets, spectra, column_planes(both // 2), row_planes(high), frame_weights(width, parts, padded))
    out = pl.pallas_call(
        functools.partial(kernel, parts, strips),
        out_shape=jax.ShapeDtypeStruct((width, frames, high), f32),
        in_specs=[pl.BlockSpec(memory_space=pltpu.HBM)] * 5,
        out_specs=pl.BlockSpec(memory_space=pltpu.VMEM),
        scratch_shapes=[pltpu.SMEM(offsets.shape, offsets.dtype)]
        + [pltpu.VMEM(operand.shape, operand.dtype) for operand in operands[1:]]
        + [
            pltpu.VMEM((COLS, 2 * depth), f32),
            pltpu.VMEM((COLS, 2 * depth), f32),
            pltpu.VMEM((parts, 8, 2 * depth), f32),
            pltpu.VMEM((parts, 2 * width // 4 + 1, 4, 2 * depth), bf16),
            pltpu.VMEM((strips, parts, 2 * width // 4 + 1, 4, 2 * depth), bf16),
            pltpu.VMEM((total_rows, 2 * KR), bf16),
            pltpu.VMEM((total_rows, high), f32),
            pltpu.VMEM((padded, high), bf16),
            pltpu.SemaphoreType.DMA((5,)),
            pltpu.SemaphoreType.DMA((1,)),
            pltpu.SemaphoreType.DMA((parts,)),
            pltpu.SemaphoreType.DMA((parts,)),
            pltpu.SemaphoreType.DMA((parts,)),
            pltpu.SemaphoreType.DMA((parts,)),
        ],
        compiler_params=pltpu.CompilerParams(collective_id=0, has_side_effects=True, vmem_limit_bytes=48 << 20),
        name="sar",
    )(*(pltpu.with_memory_space_constraint(operand, pltpu.HBM) for operand in operands))
    return jnp.transpose(out, (2, 0, 1))


def fits(mesh):
    parts, strips = mesh.shape["sub"], mesh.shape["strip"]
    return strips == 2 and KR // strips == LANES and COLS % parts == 0 and COLS // parts == 16 and parts % 4 == 0


def body(mesh, spectra, offsets):
    if fits(mesh) and spectra.shape[0] == 2:
        return kernel_body(spectra, offsets)
    return plain_body(spectra, offsets)


def solution(mesh):
    in_specs = (P("sub", "strip", None), P("sub"))
    out_specs = P("strip", "sub", None)
    return jax.shard_map(
        functools.partial(body, mesh), mesh=mesh, in_specs=in_specs, out_specs=out_specs, check_vma=False
    )
```

```python
import functools
import math

import jax
import jax.numpy as jnp
import numpy as np
from jax import lax
from jax.experimental import pallas as pl
from jax.experimental.pallas import tpu as pltpu
from jax.sharding import PartitionSpec as P

KR = 256
ROWS = 1024
COLS = 256
WIN = 8
BG = 16


def column_table(samples, parts):
    wide = COLS // parts + 2
    column = (np.arange(parts) * (wide - 2))[:, None] + np.arange(-1, wide - 1)[None, :]
    inside = (column >= 0) & (column < COLS)
    phase = ((np.arange(samples)[:, None, None] * column[None]) % samples) * (2.0 * math.pi / samples)
    cosine = np.where(inside, np.cos(phase), 0.0) / math.sqrt(samples)
    sine = np.where(inside, -np.sin(phase), 0.0) / math.sqrt(samples)
    upper = np.stack([cosine, sine], axis=2)
    lower = np.stack([-sine, cosine], axis=2)
    return jnp.asarray(np.concatenate([upper, lower], axis=0).astype(np.float32)).astype(jnp.bfloat16)


def row_table(rows):
    sample = jnp.arange(KR, dtype=jnp.int32)[:, None] - KR // 2
    phase = jnp.mod(rows[None, :] * sample, ROWS).astype(jnp.float32) * (2.0 * math.pi / ROWS)
    scale = jnp.where((rows >= 0) & (rows < ROWS), 1.0 / math.sqrt(KR), 0.0)[None, :]
    cosine = jnp.cos(phase) * scale
    sine = jnp.sin(phase) * scale
    upper = jnp.stack([cosine, sine], axis=1)
    lower = jnp.stack([-sine, cosine], axis=1)
    return jnp.concatenate([upper, lower], axis=0).astype(jnp.bfloat16)


def rotation(offsets, samples):
    angle = jnp.mod(offsets[:, None] * (samples[None, :] - KR // 2), ROWS).astype(jnp.float32) * (2.0 * math.pi / ROWS)
    return jnp.cos(angle), jnp.sin(angle)


def plain_body(spectra, offsets):
    own, depth = spectra.shape[:2]
    parts, strips = lax.axis_size("sub"), lax.axis_size("strip")
    wide = COLS // parts + 2
    high = ROWS // strips
    strip = lax.axis_index("strip")
    frames = own * parts
    table = column_table(spectra.shape[2] // 2, parts)
    cosine, sine = rotation(offsets, strip * depth + jnp.arange(depth, dtype=jnp.int32))
    mixed = jnp.einsum("skc,cdpn->dspnk", spectra, table, preferred_element_type=jnp.float32)
    real, imag = mixed[:, :, 0], mixed[:, :, 1]
    cosine, sine = cosine[None, :, None, :], sine[None, :, None, :]
    shifted = jnp.stack([real * cosine - imag * sine, real * sine + imag * cosine], axis=2).astype(jnp.bfloat16)
    held = lax.all_to_all(shifted, "sub", split_axis=0, concat_axis=0, tiled=True)
    held = held.reshape(frames, 2, wide, depth)
    whole = jnp.zeros((frames, 2, wide, strips, depth), jnp.bfloat16)
    for step in range(strips):
        part = held
        if step:
            part = lax.ppermute(held, "strip", [(i, (i + step) % strips) for i in range(strips)])
        source = jnp.mod(strip - step, strips)
        whole = lax.dynamic_update_slice(whole, part[:, :, :, None], (0, 0, 0, source, 0))
    wider = whole.reshape(frames, 2, wide, KR).astype(jnp.float32)
    summed = wider
    for lead in range(1, WIN):
        summed = summed + jnp.roll(wider, -lead, axis=0)
    rows = strip * high + jnp.arange(-1, high + 1, dtype=jnp.int32)
    product = jnp.einsum(
        "fpnk,pkqm->qnfm",
        summed.astype(jnp.bfloat16),
        row_table(rows).reshape(2, KR, 2, high + 2),
        preferred_element_type=jnp.float32,
    )
    log_power = jnp.log(1.0 + product[0] * product[0] + product[1] * product[1])
    total = log_power[:, :, :-2] + log_power[:, :, 1:-1] + log_power[:, :, 2:]
    filtered = (total[:-2] + total[1:-1] + total[2:]) / 9.0
    background = filtered
    for behind in range(1, BG):
        background = background + jnp.roll(filtered, behind, axis=1)
    return jnp.transpose(filtered - background / BG, (2, 0, 1))


LANES = 128
GROUP = 4
RADIX = 4
LAYERS = 4
MESH = pl.DeviceIdType.MESH


def column_planes(samples):
    phase = (np.arange(COLS)[:, None] * np.arange(samples // RADIX)[None, :] % samples) * (2.0 * math.pi / samples)
    cosine, sine = np.cos(phase) / math.sqrt(samples), -np.sin(phase) / math.sqrt(samples)
    planes = np.block([[[cosine, -sine]], [[sine, cosine]]])
    planes = planes.reshape(2, COLS // RADIX, RADIX, 2 * samples // RADIX).transpose(2, 0, 1, 3)
    planes = planes.reshape(RADIX, 2 * COLS // RADIX, 2 * samples // RADIX)
    return jnp.asarray(planes.astype(np.float32).astype(jnp.bfloat16))


def row_planes(high):
    row = np.concatenate([np.arange(high + LANES - 1), [-1]])
    used = (row <= high)[None, :]
    phase = (row[None, :] * (2 * np.arange(KR // 2)[:, None] + 1) % (2 * ROWS)) * (math.pi / ROWS)
    planes = np.concatenate([np.cos(phase) * used, -np.sin(phase) * used]) / math.sqrt(KR)
    return jnp.asarray(planes.astype(np.float32).astype(jnp.bfloat16))


def stages(upper):
    return [[2 * upper], [LAYERS - 1], [1 - upper, 2 - upper]]


def frame_weights(width, sources, rows):
    frames = 2 * sources
    weights = np.zeros((2, width, frames, rows), np.float32)
    target = np.arange(frames)

    def place(upper, at, column, frame):
        series = np.where(target == frame, 1.0, 0.0) - np.where((target - frame) % frames < BG, 1.0 / BG, 0.0)
        for near in range(max(column - 1, 0), min(column + 2, width)):
            weights[upper, near, :, at] = series

    for upper in range(2):
        at, edge_at = 0, frames * width
        for group in stages(upper):
            held = [layer * GROUP + index for layer in group for index in range(GROUP)]
            for lane in range(2):
                for source in held:
                    for spot in range(width):
                        place(upper, at, RADIX * (spot % (width // RADIX)) + spot // (width // RADIX), 2 * source + lane)
                        at += 1
            for lane in range(2):
                for source in held:
                    for side in range(2):
                        place(upper, edge_at, (-1, width)[side], 2 * source + lane)
                        edge_at += 1
    return jnp.asarray(weights.reshape(2, width * frames, rows).astype(jnp.bfloat16))


def product_of(a, b):
    return lax.dot_general(a, b, (((1,), (0,)), ((), ())), preferred_element_type=jnp.float32)


def product_t(a, b):
    return lax.dot_general(a, b, (((1,), (1,)), ((), ())), preferred_element_type=jnp.float32)


def kernel(
    parts, strips, offsets_hbm, spectra_hbm, columns_hbm, rows_hbm, weights_hbm, out_ref,
    offsets_ref, spectra, columns, rows, weights, mixed, ends, edge, main, held, lhs, boxed, level,
    load_sem, own_sem, send_sem, recv_sem, pass_sem, got_sem,
):
    me, strip = lax.axis_index("sub"), lax.axis_index("strip")
    width = COLS // parts
    depth = spectra.shape[1]
    samples = spectra.shape[2] // 2
    high = out_ref.shape[2]
    other = 1 - strip
    reach = LAYERS // 2
    layer, place = me // GROUP, lax.rem(me, GROUP)
    upper, within = layer // reach, lax.rem(layer, reach)

    def device_at(half, step, turn):
        return (half * reach + step) * GROUP + lax.rem(place + turn + GROUP, GROUP)

    close = [device_at(upper, within, turn) for turn in range(1, GROUP)]
    close += [
        device_at(upper, lax.rem(within + step, reach), turn) for step in range(1, reach) for turn in range(GROUP)
    ]
    outward = [(1 - upper) * (reach - 1) + (2 * upper - 1) * step for step in range(reach)]
    targets = [device_at(1 - upper, step, turn) for step in outward for turn in range(GROUP)]
    origins = [device_at(1 - upper, step, -turn) for step in outward for turn in range(GROUP)]

    def load(source, target, i):
        return pltpu.make_async_copy(source, target, load_sem.at[i])

    loads = [
        load(offsets_hbm, offsets_ref, 0),
        load(spectra_hbm.at[0], spectra.at[0], 1),
        load(spectra_hbm.at[1], spectra.at[1], 2),
        load(columns_hbm, columns, 3),
        load(rows_hbm, rows, 4),
        load(weights_hbm.at[upper], weights, 5),
    ]
    for copy in loads[:4]:
        copy.start()
    barrier = pltpu.get_barrier_semaphore()
    for away in range(1, parts):
        pl.semaphore_signal(barrier, inc=1, device_id=(lax.rem(me + away, parts), strip), device_id_type=MESH)
    for near in [me] + close:
        pl.semaphore_signal(barrier, inc=1, device_id=(near, other), device_id_type=MESH)

    loads[0].wait()
    lane = lax.broadcasted_iota(jnp.int32, (1, 2 * depth), 1)
    sample = strip * depth + jnp.where(lane < depth, lane, lane - depth) - KR // 2
    offset = jnp.where(lane < depth, offsets_ref[0], offsets_ref[1])
    angle = jnp.bitwise_and(offset * sample, ROWS - 1).astype(jnp.float32) * (2.0 * math.pi / ROWS)
    cosine, sine = jnp.cos(angle), jnp.sin(angle)
    edge[...] = jnp.zeros_like(edge)
    quarter = samples // RADIX
    for own in range(2):
        loads[1 + own].wait()
        re = [spectra[own, :, p * quarter : (p + 1) * quarter].astype(jnp.float32) for p in range(RADIX)]
        im = [spectra[own, :, samples + p * quarter : samples + (p + 1) * quarter].astype(jnp.float32) for p in range(RADIX)]
        even_re, even_im, gap_re, gap_im = re[0] + re[2], im[0] + im[2], re[0] - re[2], im[0] - im[2]
        odd_re, odd_im, turn_re, turn_im = re[1] + re[3], im[1] + im[3], im[1] - im[3], re[3] - re[1]
        folded = [
            (even_re + odd_re, even_im + odd_im), (gap_re + turn_re, gap_im + turn_im),
            (even_re - odd_re, even_im - odd_im), (gap_re - turn_re, gap_im - turn_im),
        ]
        for residue, pair in enumerate(folded):
            for part, value in enumerate(pair):
                mixed[residue, own * depth : (own + 1) * depth, part * quarter : (part + 1) * quarter] = value.astype(jnp.bfloat16)
    loads[3].wait()
    for copy in loads[4:]:
        copy.start()
    rank = COLS // RADIX
    slots = width // RADIX
    back = lax.broadcasted_iota(jnp.int32, (rank, depth), 1)
    back = (1 - strip) * (depth - 1 - 2 * back) + back
    for residue in range(RADIX):
        both = product_t(columns[residue], mixed[residue])
        re, im = both[:rank], both[rank:]
        for part, value in ((0, re * cosine - im * sine), (1, re * sine + im * cosine)):
            for own in range(2):
                turned = jnp.take_along_axis(value[:, own * depth : (own + 1) * depth], back, axis=1, mode="promise_in_bounds")
                into = slice(part * depth, (part + 1) * depth)
                if residue == 0:
                    ends[2 * own + 1, :, into] = turned
                if residue == RADIX - 1:
                    ends[2 * own, :, into] = turned
                main[:, own * RADIX + residue, :, into] = (
                    turned.reshape(parts, slots, depth).astype(jnp.bfloat16)
                )
    for own in range(2):
        for d in range(parts):
            if d > 0:
                edge[d, 2 * own : 2 * own + 1] = ends[2 * own, d * slots - 1 : d * slots]
            if d < parts - 1:
                edge[d, 2 * own + 1 : 2 * own + 2] = ends[2 * own + 1, (d + 1) * slots : (d + 1) * slots + 1]
    main[:, 2 * RADIX] = edge[:, :4].astype(jnp.bfloat16)

    pl.semaphore_wait(barrier, parts + len(close))

    def send(to):
        return pltpu.make_async_remote_copy(
            src_ref=main.at[to], dst_ref=held.at[strip, me], send_sem=send_sem.at[to],
            recv_sem=recv_sem.at[me], device_id=(to, strip), device_id_type=MESH,
        )

    def arrival(h, source, sem):
        return pltpu.make_async_remote_copy(
            src_ref=main.at[source], dst_ref=held.at[h, source], send_sem=send_sem.at[source],
            recv_sem=sem.at[source], device_id=(source, strip), device_id_type=MESH,
        )

    def cross(to):
        return pltpu.make_async_remote_copy(
            src_ref=main.at[to], dst_ref=held.at[strip, me], send_sem=pass_sem.at[to],
            recv_sem=got_sem.at[me], device_id=(to, other), device_id_type=MESH,
        )

    def forward(source):
        return pltpu.make_async_remote_copy(
            src_ref=held.at[strip, source], dst_ref=held.at[strip, source], send_sem=pass_sem.at[source],
            recv_sem=got_sem.at[source], device_id=(me, other), device_id_type=MESH,
        )

    for to, near in zip(targets, [me] + close):
        send(to).start()
        cross(near).start()
    for to in close:
        send(to).start()
    kept = pltpu.make_async_copy(main.at[me], held.at[strip, me], own_sem.at[0])
    kept.start()

    alternate = 1.0 - 2.0 * lax.rem(lax.broadcasted_iota(jnp.int32, (1, 1, 2 * depth), 2), 2).astype(jnp.float32)
    signs = [1.0 - strip * (1.0 + alternate), 1.0 - strip * (1.0 - alternate)]
    row_at = lax.broadcasted_iota(jnp.int32, (GROUP, 8, 2 * depth), 1)

    def window(h, first, count):
        block = []
        for step in range(count + 1):
            at = lax.rem(first + step, LAYERS) * GROUP
            block.append(held[h, pl.ds(at, GROUP)].astype(jnp.float32) * signs[h][None])
        whole = jnp.concatenate(block, axis=0)
        number = count * GROUP
        body = whole[:, : 2 * RADIX].reshape(number + GROUP, 2 * width, 2 * depth)
        near = whole[:, 2 * RADIX]
        near = jnp.concatenate([near, jnp.zeros_like(near)], axis=1)
        near_second = jnp.concatenate([pltpu.roll(near[i], 6, 0)[None] for i in range(number + GROUP)], axis=0)
        results = []
        for one, two in ((body[:, :width], body[:, width:]), (near, near_second)):
            pair = one + two
            double = pair[:-1] + pair[1:]
            quad = double[:number] + double[2 : number + 2]
            results.append((quad, quad - one[:number] + one[WIN // 2 : number + WIN // 2]))
        packed = []
        for frame in results[1]:
            for group in range(count):
                masked = jnp.where(row_at < 2, frame[GROUP * group : GROUP * (group + 1)], 0.0)
                total = masked[0]
                for j in range(1, GROUP):
                    total = total + pltpu.roll(masked[j], 2 * j, 0)
                packed.append(total)
        flat = [frame.reshape(number * width, 2 * depth) for frame in results[0]]
        return jnp.concatenate(flat + packed, axis=0)

    tail = lax.broadcasted_iota(jnp.int32, (1, high + LANES), 1)
    outside = ((tail == high) & (strip == strips - 1)) | ((tail == high + LANES - 1) & (strip == 0))
    inside = jnp.where(outside, 0.0, 1.0)

    def image(lower_half, upper_half):
        total = upper_half + lower_half
        gap = upper_half - lower_half
        size = total.shape[0]
        lhs[:size, :depth] = total[:, :depth].astype(jnp.bfloat16)
        lhs[:size, depth:] = gap[:, depth:].astype(jnp.bfloat16)
        lhs[size : 2 * size, :depth] = total[:, depth:].astype(jnp.bfloat16)
        lhs[size : 2 * size, depth:] = (-gap[:, :depth]).astype(jnp.bfloat16)
        step = size // 2
        pieces = []
        for at in range(0, size, step):
            re = product_of(lhs[at : at + step], rows[...])
            im = product_of(lhs[size + at : size + at + step], rows[...])
            power = jnp.log(1.0 + re * re + im * im) * inside
            pieces.append((power + pltpu.roll(power, 1, 1) + pltpu.roll(power, high + LANES - 1, 1))[:, :high])
        return pieces

    batch = GROUP * width
    for source in origins[:GROUP]:
        arrival(strip, source, recv_sem).wait_recv()
        forward(source).start()
    for source in close:
        arrival(strip, source, recv_sem).wait_recv()
    kept.wait()
    for source in [me] + close:
        arrival(other, source, got_sem).wait_recv()
    loads[4].wait()
    pieces = image(window(0, 2 * upper, 1), window(1, 2 * upper, 1))
    size = 2 * batch + 2 * 8
    for i, piece in enumerate(pieces):
        boxed[0, i * (size // 2) : (i + 1) * (size // 2)] = piece
    for source in origins[GROUP:]:
        arrival(strip, source, recv_sem).wait_recv()
        forward(source).start()
    for source in origins[:GROUP]:
        arrival(other, source, got_sem).wait_recv()
    pieces = image(window(0, LAYERS - 1, 1), window(1, LAYERS - 1, 1))
    for i, piece in enumerate(pieces):
        boxed[1, i * (size // 2) : (i + 1) * (size // 2)] = piece
    early = boxed[:, : 2 * batch].reshape(2, 2 * GROUP, width, high)
    mean = jnp.sum(jnp.sum(early, axis=0), axis=0) * (1.0 / (4 * GROUP))
    for i in range(2):
        level[2 * batch * i : 2 * batch * (i + 1)] = (early[i] - mean[None]).reshape(2 * batch, high).astype(jnp.bfloat16)
    early_near = boxed[:, 2 * batch : size].reshape(4, 8, high)
    near_mean = jnp.sum(early_near, axis=0) * (1.0 / (4 * GROUP))
    near_mean = near_mean + pltpu.roll(near_mean, 4, 0)
    near_mean = near_mean + pltpu.roll(near_mean, 2, 0)
    top = 2 * parts * width
    level[top : top + 32] = (early_near - near_mean[None]).reshape(32, high).astype(jnp.bfloat16)
    level[top + 64 :] = jnp.zeros((level.shape[0] - top - 64, high), jnp.bfloat16)

    for source in origins[GROUP:]:
        arrival(other, source, got_sem).wait_recv()
    pieces = image(window(0, 1 - upper, 2), window(1, 1 - upper, 2))
    late = jnp.concatenate(pieces, axis=0)
    block = late[: 4 * batch].reshape(4 * GROUP, width, high)
    level[4 * batch : 8 * batch] = (block - mean[None]).reshape(4 * batch, high).astype(jnp.bfloat16)
    near = late[4 * batch :].reshape(4, 8, high)
    level[top + 32 : top + 64] = (near - near_mean[None]).reshape(32, high).astype(jnp.bfloat16)
    loads[5].wait()
    frames = 2 * parts
    for c in range(0, width, 4):
        piece = product_of(weights[c * frames : (c + 4) * frames], level[...])
        out_ref[c : c + 4] = (piece * (1.0 / 9.0)).reshape(4, frames, high)
    for to in targets + close:
        send(to).wait_send()
    for to in [me] + close:
        cross(to).wait_send()
    for source in origins:
        forward(source).wait_send()


def kernel_body(spectra, offsets):
    parts, strips = lax.axis_size("sub"), lax.axis_size("strip")
    own, depth, both = spectra.shape
    width, high = COLS // parts, ROWS // strips
    frames = own * parts
    total_rows = frames * (width + 2)
    padded = -(-total_rows // LANES) * LANES
    bf16, f32 = jnp.bfloat16, jnp.float32
    operands = (offsets, spectra, column_planes(both // 2), row_planes(high), frame_weights(width, parts, padded))
    shapes = [operand.shape for operand in operands[1:4]] + [operands[4].shape[1:]]
    half = 2 * GROUP * width + 2 * 8
    out = pl.pallas_call(
        functools.partial(kernel, parts, strips),
        out_shape=jax.ShapeDtypeStruct((width, frames, high), f32),
        in_specs=[pl.BlockSpec(memory_space=pltpu.HBM)] * 5,
        out_specs=pl.BlockSpec(memory_space=pltpu.VMEM),
        scratch_shapes=[pltpu.SMEM(offsets.shape, offsets.dtype)]
        + [pltpu.VMEM(shape, bf16) for shape in shapes]
        + [
            pltpu.VMEM((RADIX, 2 * depth, both // RADIX), bf16),
            pltpu.VMEM((4, COLS // RADIX, 2 * depth), f32),
            pltpu.VMEM((parts, 8, 2 * depth), f32),
            pltpu.VMEM((parts, 2 * RADIX + 1, width // RADIX, 2 * depth), bf16),
            pltpu.VMEM((strips, parts, 2 * RADIX + 1, width // RADIX, 2 * depth), bf16),
            pltpu.VMEM((4 * half, KR), bf16),
            pltpu.VMEM((2, half, high), f32),
            pltpu.VMEM((padded, high), bf16),
            pltpu.SemaphoreType.DMA((6,)),
            pltpu.SemaphoreType.DMA((1,)),
            pltpu.SemaphoreType.DMA((parts,)),
            pltpu.SemaphoreType.DMA((parts,)),
            pltpu.SemaphoreType.DMA((parts,)),
            pltpu.SemaphoreType.DMA((parts,)),
        ],
        compiler_params=pltpu.CompilerParams(collective_id=0, has_side_effects=True, vmem_limit_bytes=48 << 20),
        name="sar",
    )(*(pltpu.with_memory_space_constraint(operand, pltpu.HBM) for operand in operands))
    return jnp.transpose(out, (2, 0, 1))


def fits(mesh):
    parts, strips = mesh.shape["sub"], mesh.shape["strip"]
    return strips == 2 and KR // strips == LANES and COLS % parts == 0 and COLS // parts == 16 and parts == LAYERS * GROUP


def body(mesh, spectra, offsets):
    if fits(mesh) and spectra.shape[0] == 2:
        return kernel_body(spectra, offsets)
    return plain_body(spectra, offsets)


def solution(mesh):
    in_specs = (P("sub", "strip", None), P("sub"))
    out_specs = P("strip", "sub", None)
    return jax.shard_map(
        functools.partial(body, mesh), mesh=mesh, in_specs=in_specs, out_specs=out_specs, check_vma=False
    )
```

```python
import functools
import math

import jax
import jax.numpy as jnp
import numpy as np
from jax import lax
from jax.experimental import pallas as pl
from jax.experimental.pallas import tpu as pltpu
from jax.sharding import PartitionSpec as P

KR = 256
ROWS = 1024
COLS = 256
WIN = 8
BG = 16


def column_table(samples, parts):
    wide = COLS // parts + 2
    column = (np.arange(parts) * (wide - 2))[:, None] + np.arange(-1, wide - 1)[None, :]
    inside = (column >= 0) & (column < COLS)
    phase = ((np.arange(samples)[:, None, None] * column[None]) % samples) * (2.0 * math.pi / samples)
    cosine = np.where(inside, np.cos(phase), 0.0) / math.sqrt(samples)
    sine = np.where(inside, -np.sin(phase), 0.0) / math.sqrt(samples)
    upper = np.stack([cosine, sine], axis=2)
    lower = np.stack([-sine, cosine], axis=2)
    return jnp.asarray(np.concatenate([upper, lower], axis=0).astype(np.float32)).astype(jnp.bfloat16)


def row_table(rows):
    sample = jnp.arange(KR, dtype=jnp.int32)[:, None] - KR // 2
    phase = jnp.mod(rows[None, :] * sample, ROWS).astype(jnp.float32) * (2.0 * math.pi / ROWS)
    scale = jnp.where((rows >= 0) & (rows < ROWS), 1.0 / math.sqrt(KR), 0.0)[None, :]
    cosine = jnp.cos(phase) * scale
    sine = jnp.sin(phase) * scale
    upper = jnp.stack([cosine, sine], axis=1)
    lower = jnp.stack([-sine, cosine], axis=1)
    return jnp.concatenate([upper, lower], axis=0).astype(jnp.bfloat16)


def rotation(offsets, samples):
    angle = jnp.mod(offsets[:, None] * (samples[None, :] - KR // 2), ROWS).astype(jnp.float32) * (2.0 * math.pi / ROWS)
    return jnp.cos(angle), jnp.sin(angle)


def plain_body(spectra, offsets):
    own, depth = spectra.shape[:2]
    parts, strips = lax.axis_size("sub"), lax.axis_size("strip")
    wide = COLS // parts + 2
    high = ROWS // strips
    strip = lax.axis_index("strip")
    frames = own * parts
    table = column_table(spectra.shape[2] // 2, parts)
    cosine, sine = rotation(offsets, strip * depth + jnp.arange(depth, dtype=jnp.int32))
    mixed = jnp.einsum("skc,cdpn->dspnk", spectra, table, preferred_element_type=jnp.float32)
    real, imag = mixed[:, :, 0], mixed[:, :, 1]
    cosine, sine = cosine[None, :, None, :], sine[None, :, None, :]
    shifted = jnp.stack([real * cosine - imag * sine, real * sine + imag * cosine], axis=2).astype(jnp.bfloat16)
    held = lax.all_to_all(shifted, "sub", split_axis=0, concat_axis=0, tiled=True)
    held = held.reshape(frames, 2, wide, depth)
    whole = jnp.zeros((frames, 2, wide, strips, depth), jnp.bfloat16)
    for step in range(strips):
        part = held
        if step:
            part = lax.ppermute(held, "strip", [(i, (i + step) % strips) for i in range(strips)])
        source = jnp.mod(strip - step, strips)
        whole = lax.dynamic_update_slice(whole, part[:, :, :, None], (0, 0, 0, source, 0))
    wider = whole.reshape(frames, 2, wide, KR).astype(jnp.float32)
    summed = wider
    for lead in range(1, WIN):
        summed = summed + jnp.roll(wider, -lead, axis=0)
    rows = strip * high + jnp.arange(-1, high + 1, dtype=jnp.int32)
    product = jnp.einsum(
        "fpnk,pkqm->qnfm",
        summed.astype(jnp.bfloat16),
        row_table(rows).reshape(2, KR, 2, high + 2),
        preferred_element_type=jnp.float32,
    )
    log_power = jnp.log(1.0 + product[0] * product[0] + product[1] * product[1])
    total = log_power[:, :, :-2] + log_power[:, :, 1:-1] + log_power[:, :, 2:]
    filtered = (total[:-2] + total[1:-1] + total[2:]) / 9.0
    background = filtered
    for behind in range(1, BG):
        background = background + jnp.roll(filtered, behind, axis=1)
    return jnp.transpose(filtered - background / BG, (2, 0, 1))


LANES = 128
GROUP = 4
RADIX = 4
LAYERS = 4
MESH = pl.DeviceIdType.MESH


def column_planes(samples):
    phase = (np.arange(COLS)[:, None] * np.arange(samples // RADIX)[None, :] % samples) * (2.0 * math.pi / samples)
    cosine, sine = np.cos(phase) / math.sqrt(samples), -np.sin(phase) / math.sqrt(samples)
    planes = np.block([[[cosine, -sine]], [[sine, cosine]]])
    planes = planes.reshape(2, COLS // RADIX, RADIX, 2 * samples // RADIX).transpose(2, 0, 1, 3)
    planes = planes.reshape(RADIX, 2 * COLS // RADIX, 2 * samples // RADIX)
    return jnp.asarray(planes.astype(np.float32).astype(jnp.bfloat16))


def row_planes(high):
    row = np.concatenate([np.arange(high + LANES - 1), [-1]])
    used = (row <= high)[None, :]
    phase = (row[None, :] * (2 * np.arange(KR // 2)[:, None] + 1) % (2 * ROWS)) * (math.pi / ROWS)
    planes = np.concatenate([np.cos(phase) * used, -np.sin(phase) * used]) / math.sqrt(KR)
    return jnp.asarray(planes.astype(np.float32).astype(jnp.bfloat16))


def stages(upper):
    return [[2 * upper], [LAYERS - 1], [1 - upper, 2 - upper]]


def frame_weights(width, sources, rows):
    frames = 2 * sources
    weights = np.zeros((2, width, frames, rows), np.float32)
    target = np.arange(frames)

    def place(upper, at, column, frame):
        series = np.where(target == frame, 1.0, 0.0) - np.where((target - frame) % frames < BG, 1.0 / BG, 0.0)
        for near in range(max(column - 1, 0), min(column + 2, width)):
            weights[upper, near, :, at] = series

    for upper in range(2):
        at, edge_at = 0, frames * width
        for group in stages(upper):
            held = [layer * GROUP + index for layer in group for index in range(GROUP)]
            for lane in range(2):
                for source in held:
                    for spot in range(width):
                        place(upper, at, RADIX * (spot % (width // RADIX)) + spot // (width // RADIX), 2 * source + lane)
                        at += 1
            for lane in range(2):
                for source in held:
                    for side in range(2):
                        place(upper, edge_at, (-1, width)[side], 2 * source + lane)
                        edge_at += 1
    return jnp.asarray(weights.reshape(2, width * frames, rows).astype(jnp.bfloat16))


def product_of(a, b):
    return lax.dot_general(a, b, (((1,), (0,)), ((), ())), preferred_element_type=jnp.float32)


def product_t(a, b):
    return lax.dot_general(a, b, (((1,), (1,)), ((), ())), preferred_element_type=jnp.float32)


def kernel(
    parts, strips, offsets_hbm, spectra_hbm, columns_hbm, rows_hbm, weights_hbm, out_ref,
    offsets_ref, spectra, columns, rows, weights, mixed, ends, edge, main, held, lhs, boxed, level,
    load_sem, own_sem, send_sem, recv_sem, pass_sem, got_sem,
):
    me, strip = lax.axis_index("sub"), lax.axis_index("strip")
    width = COLS // parts
    depth = spectra.shape[1]
    samples = spectra.shape[2] // 2
    high = out_ref.shape[2]
    other = 1 - strip
    reach = LAYERS // 2
    layer, place = me // GROUP, lax.rem(me, GROUP)
    upper, within = layer // reach, lax.rem(layer, reach)

    def device_at(half, step, turn):
        return (half * reach + step) * GROUP + lax.rem(place + turn + GROUP, GROUP)

    close = [device_at(upper, within, turn) for turn in range(1, GROUP)]
    close += [
        device_at(upper, lax.rem(within + step, reach), turn) for step in range(1, reach) for turn in range(GROUP)
    ]
    outward = [(1 - upper) * (reach - 1) + (2 * upper - 1) * step for step in range(reach)]
    targets = [device_at(1 - upper, step, turn) for step in outward for turn in range(GROUP)]
    origins = [device_at(1 - upper, step, -turn) for step in outward for turn in range(GROUP)]

    def load(source, target, i):
        return pltpu.make_async_copy(source, target, load_sem.at[i])

    loads = [
        load(offsets_hbm, offsets_ref, 0),
        load(spectra_hbm.at[0], spectra.at[0], 1),
        load(spectra_hbm.at[1], spectra.at[1], 2),
        load(columns_hbm, columns, 3),
        load(rows_hbm, rows, 4),
        load(weights_hbm.at[upper], weights, 5),
    ]
    for copy in loads[:4]:
        copy.start()
    barrier = pltpu.get_barrier_semaphore()
    for away in range(1, parts):
        pl.semaphore_signal(barrier, inc=1, device_id=(lax.rem(me + away, parts), strip), device_id_type=MESH)
    for near in [me] + close:
        pl.semaphore_signal(barrier, inc=1, device_id=(near, other), device_id_type=MESH)

    loads[0].wait()
    lane = lax.broadcasted_iota(jnp.int32, (1, 2 * depth), 1)
    sample = strip * depth + jnp.where(lane < depth, lane, lane - depth) - KR // 2
    offset = jnp.where(lane < depth, offsets_ref[0], offsets_ref[1])
    angle = jnp.bitwise_and(offset * sample, ROWS - 1).astype(jnp.float32) * (2.0 * math.pi / ROWS)
    cosine, sine = jnp.cos(angle), jnp.sin(angle)
    edge[...] = jnp.zeros_like(edge)
    quarter = samples // RADIX
    for own in range(2):
        loads[1 + own].wait()
        re = [spectra[own, :, p * quarter : (p + 1) * quarter].astype(jnp.float32) for p in range(RADIX)]
        im = [spectra[own, :, samples + p * quarter : samples + (p + 1) * quarter].astype(jnp.float32) for p in range(RADIX)]
        even_re, even_im, gap_re, gap_im = re[0] + re[2], im[0] + im[2], re[0] - re[2], im[0] - im[2]
        odd_re, odd_im, turn_re, turn_im = re[1] + re[3], im[1] + im[3], im[1] - im[3], re[3] - re[1]
        folded = [
            (even_re + odd_re, even_im + odd_im), (gap_re + turn_re, gap_im + turn_im),
            (even_re - odd_re, even_im - odd_im), (gap_re - turn_re, gap_im - turn_im),
        ]
        for residue, pair in enumerate(folded):
            for part, value in enumerate(pair):
                mixed[residue, own * depth : (own + 1) * depth, part * quarter : (part + 1) * quarter] = value.astype(jnp.bfloat16)
    loads[3].wait()
    for copy in loads[4:]:
        copy.start()
    rank = COLS // RADIX
    slots = width // RADIX
    back = lax.broadcasted_iota(jnp.int32, (rank, depth), 1)
    back = (1 - strip) * (depth - 1 - 2 * back) + back
    for residue in range(RADIX):
        both = product_t(columns[residue], mixed[residue])
        re, im = both[:rank], both[rank:]
        for part, value in ((0, re * cosine - im * sine), (1, re * sine + im * cosine)):
            for own in range(2):
                turned = jnp.take_along_axis(value[:, own * depth : (own + 1) * depth], back, axis=1, mode="promise_in_bounds")
                into = slice(part * depth, (part + 1) * depth)
                if residue == 0:
                    ends[2 * own + 1, :, into] = turned
                if residue == RADIX - 1:
                    ends[2 * own, :, into] = turned
                main[:, own * RADIX + residue, :, into] = (
                    turned.reshape(parts, slots, depth).astype(jnp.bfloat16)
                )
    for own in range(2):
        for d in range(parts):
            if d > 0:
                edge[d, 2 * own : 2 * own + 1] = ends[2 * own, d * slots - 1 : d * slots]
            if d < parts - 1:
                edge[d, 2 * own + 1 : 2 * own + 2] = ends[2 * own + 1, (d + 1) * slots : (d + 1) * slots + 1]
    main[:, 2 * RADIX] = edge[:, :4].astype(jnp.bfloat16)

    pl.semaphore_wait(barrier, parts + len(close))

    def send(to):
        return pltpu.make_async_remote_copy(
            src_ref=main.at[to], dst_ref=held.at[strip, me], send_sem=send_sem.at[to],
            recv_sem=recv_sem.at[me], device_id=(to, strip), device_id_type=MESH,
        )

    def arrival(h, source, sem):
        return pltpu.make_async_remote_copy(
            src_ref=main.at[source], dst_ref=held.at[h, source], send_sem=send_sem.at[source],
            recv_sem=sem.at[source], device_id=(source, strip), device_id_type=MESH,
        )

    def cross(to):
        return pltpu.make_async_remote_copy(
            src_ref=main.at[to], dst_ref=held.at[strip, me], send_sem=pass_sem.at[to],
            recv_sem=got_sem.at[me], device_id=(to, other), device_id_type=MESH,
        )

    def forward(source):
        return pltpu.make_async_remote_copy(
            src_ref=held.at[strip, source], dst_ref=held.at[strip, source], send_sem=pass_sem.at[source],
            recv_sem=got_sem.at[source], device_id=(me, other), device_id_type=MESH,
        )

    for to, near in zip(targets, [me] + close):
        send(to).start()
        cross(near).start()
    for to in close:
        send(to).start()
    kept = pltpu.make_async_copy(main.at[me], held.at[strip, me], own_sem.at[0])
    kept.start()

    alternate = 1.0 - 2.0 * lax.rem(lax.broadcasted_iota(jnp.int32, (1, 1, 2 * depth), 2), 2).astype(jnp.float32)
    signs = [1.0 - strip * (1.0 + alternate), 1.0 - strip * (1.0 - alternate)]
    row_at = lax.broadcasted_iota(jnp.int32, (GROUP, 8, 2 * depth), 1)

    def window(h, first, count):
        block = []
        for step in range(count + 1):
            at = lax.rem(first + step, LAYERS) * GROUP
            block.append(held[h, pl.ds(at, GROUP)].astype(jnp.float32) * signs[h][None])
        whole = jnp.concatenate(block, axis=0)
        number = count * GROUP
        body = whole[:, : 2 * RADIX].reshape(number + GROUP, 2 * width, 2 * depth)
        near = whole[:, 2 * RADIX]
        near = jnp.concatenate([near, jnp.zeros_like(near)], axis=1)
        near_second = jnp.concatenate([pltpu.roll(near[i], 6, 0)[None] for i in range(number + GROUP)], axis=0)
        results = []
        for one, two in ((body[:, :width], body[:, width:]), (near, near_second)):
            pair = one + two
            double = pair[:-1] + pair[1:]
            quad = double[:number] + double[2 : number + 2]
            results.append((quad, quad - one[:number] + one[WIN // 2 : number + WIN // 2]))
        packed = []
        for frame in results[1]:
            for group in range(count):
                masked = jnp.where(row_at < 2, frame[GROUP * group : GROUP * (group + 1)], 0.0)
                total = masked[0]
                for j in range(1, GROUP):
                    total = total + pltpu.roll(masked[j], 2 * j, 0)
                packed.append(total)
        flat = [frame.reshape(number * width, 2 * depth) for frame in results[0]]
        return jnp.concatenate(flat + packed, axis=0)

    tail = lax.broadcasted_iota(jnp.int32, (1, high + LANES), 1)
    outside = ((tail == high) & (strip == strips - 1)) | ((tail == high + LANES - 1) & (strip == 0))
    inside = jnp.where(outside, 0.0, 1.0)

    def image(lower_half, upper_half):
        total = upper_half + lower_half
        gap = upper_half - lower_half
        size = total.shape[0]
        lhs[:size, :depth] = total[:, :depth].astype(jnp.bfloat16)
        lhs[:size, depth:] = gap[:, depth:].astype(jnp.bfloat16)
        lhs[size : 2 * size, :depth] = total[:, depth:].astype(jnp.bfloat16)
        lhs[size : 2 * size, depth:] = (-gap[:, :depth]).astype(jnp.bfloat16)
        step = size // 2
        pieces = []
        for at in range(0, size, step):
            re = product_of(lhs[at : at + step], rows[...])
            im = product_of(lhs[size + at : size + at + step], rows[...])
            power = jnp.log(1.0 + re * re + im * im) * inside
            pieces.append((power + pltpu.roll(power, 1, 1) + pltpu.roll(power, high + LANES - 1, 1))[:, :high])
        return pieces

    batch = GROUP * width
    for source in origins:
        arrival(strip, source, recv_sem).wait_recv()
        forward(source).start()
    for source in close:
        arrival(strip, source, recv_sem).wait_recv()
    kept.wait()
    for source in [me] + close:
        arrival(other, source, got_sem).wait_recv()
    loads[4].wait()
    pieces = image(window(0, 2 * upper, 1), window(1, 2 * upper, 1))
    size = 2 * batch + 2 * 8
    for i, piece in enumerate(pieces):
        boxed[0, i * (size // 2) : (i + 1) * (size // 2)] = piece
    for source in origins[:GROUP]:
        arrival(other, source, got_sem).wait_recv()
    pieces = image(window(0, LAYERS - 1, 1), window(1, LAYERS - 1, 1))
    for i, piece in enumerate(pieces):
        boxed[1, i * (size // 2) : (i + 1) * (size // 2)] = piece
    early = boxed[:, : 2 * batch].reshape(2, 2 * GROUP, width, high)
    mean = jnp.sum(jnp.sum(early, axis=0), axis=0) * (1.0 / (4 * GROUP))
    for i in range(2):
        level[2 * batch * i : 2 * batch * (i + 1)] = (early[i] - mean[None]).reshape(2 * batch, high).astype(jnp.bfloat16)
    early_near = boxed[:, 2 * batch : size].reshape(4, 8, high)
    near_mean = jnp.sum(early_near, axis=0) * (1.0 / (4 * GROUP))
    near_mean = near_mean + pltpu.roll(near_mean, 4, 0)
    near_mean = near_mean + pltpu.roll(near_mean, 2, 0)
    top = 2 * parts * width
    level[top : top + 32] = (early_near - near_mean[None]).reshape(32, high).astype(jnp.bfloat16)
    level[top + 64 :] = jnp.zeros((level.shape[0] - top - 64, high), jnp.bfloat16)

    for source in origins[GROUP:]:
        arrival(other, source, got_sem).wait_recv()
    pieces = image(window(0, 1 - upper, 2), window(1, 1 - upper, 2))
    late = jnp.concatenate(pieces, axis=0)
    block = late[: 4 * batch].reshape(4 * GROUP, width, high)
    level[4 * batch : 8 * batch] = (block - mean[None]).reshape(4 * batch, high).astype(jnp.bfloat16)
    near = late[4 * batch :].reshape(4, 8, high)
    level[top + 32 : top + 64] = (near - near_mean[None]).reshape(32, high).astype(jnp.bfloat16)
    loads[5].wait()
    frames = 2 * parts
    for c in range(0, width, 4):
        piece = product_of(weights[c * frames : (c + 4) * frames], level[...])
        out_ref[c : c + 4] = (piece * (1.0 / 9.0)).reshape(4, frames, high)
    for to in targets + close:
        send(to).wait_send()
    for to in [me] + close:
        cross(to).wait_send()
    for source in origins:
        forward(source).wait_send()


def kernel_body(spectra, offsets):
    parts, strips = lax.axis_size("sub"), lax.axis_size("strip")
    own, depth, both = spectra.shape
    width, high = COLS // parts, ROWS // strips
    frames = own * parts
    total_rows = frames * (width + 2)
    padded = -(-total_rows // LANES) * LANES
    bf16, f32 = jnp.bfloat16, jnp.float32
    operands = (offsets, spectra, column_planes(both // 2), row_planes(high), frame_weights(width, parts, padded))
    shapes = [operand.shape for operand in operands[1:4]] + [operands[4].shape[1:]]
    half = 2 * GROUP * width + 2 * 8
    out = pl.pallas_call(
        functools.partial(kernel, parts, strips),
        out_shape=jax.ShapeDtypeStruct((width, frames, high), f32),
        in_specs=[pl.BlockSpec(memory_space=pltpu.HBM)] * 5,
        out_specs=pl.BlockSpec(memory_space=pltpu.VMEM),
        scratch_shapes=[pltpu.SMEM(offsets.shape, offsets.dtype)]
        + [pltpu.VMEM(shape, bf16) for shape in shapes]
        + [
            pltpu.VMEM((RADIX, 2 * depth, both // RADIX), bf16),
            pltpu.VMEM((4, COLS // RADIX, 2 * depth), f32),
            pltpu.VMEM((parts, 8, 2 * depth), f32),
            pltpu.VMEM((parts, 2 * RADIX + 1, width // RADIX, 2 * depth), bf16),
            pltpu.VMEM((strips, parts, 2 * RADIX + 1, width // RADIX, 2 * depth), bf16),
            pltpu.VMEM((4 * half, KR), bf16),
            pltpu.VMEM((2, half, high), f32),
            pltpu.VMEM((padded, high), bf16),
            pltpu.SemaphoreType.DMA((6,)),
            pltpu.SemaphoreType.DMA((1,)),
            pltpu.SemaphoreType.DMA((parts,)),
            pltpu.SemaphoreType.DMA((parts,)),
            pltpu.SemaphoreType.DMA((parts,)),
            pltpu.SemaphoreType.DMA((parts,)),
        ],
        compiler_params=pltpu.CompilerParams(collective_id=0, has_side_effects=True, vmem_limit_bytes=48 << 20),
        name="sar",
    )(*(pltpu.with_memory_space_constraint(operand, pltpu.HBM) for operand in operands))
    return jnp.transpose(out, (2, 0, 1))


def fits(mesh):
    parts, strips = mesh.shape["sub"], mesh.shape["strip"]
    return strips == 2 and KR // strips == LANES and COLS % parts == 0 and COLS // parts == 16 and parts == LAYERS * GROUP


def body(mesh, spectra, offsets):
    if fits(mesh) and spectra.shape[0] == 2:
        return kernel_body(spectra, offsets)
    return plain_body(spectra, offsets)


def solution(mesh):
    in_specs = (P("sub", "strip", None), P("sub"))
    out_specs = P("strip", "sub", None)
    return jax.shard_map(
        functools.partial(body, mesh), mesh=mesh, in_specs=in_specs, out_specs=out_specs, check_vma=False
    )
```

```python
import functools
import math

import jax
import jax.numpy as jnp
import numpy as np
from jax import lax
from jax.experimental import pallas as pl
from jax.experimental.pallas import tpu as pltpu
from jax.sharding import PartitionSpec as P

KR = 256
ROWS = 1024
COLS = 256
WIN = 8
BG = 16


def column_table(samples, parts):
    wide = COLS // parts + 2
    column = (np.arange(parts) * (wide - 2))[:, None] + np.arange(-1, wide - 1)[None, :]
    inside = (column >= 0) & (column < COLS)
    phase = ((np.arange(samples)[:, None, None] * column[None]) % samples) * (2.0 * math.pi / samples)
    cosine = np.where(inside, np.cos(phase), 0.0) / math.sqrt(samples)
    sine = np.where(inside, -np.sin(phase), 0.0) / math.sqrt(samples)
    upper = np.stack([cosine, sine], axis=2)
    lower = np.stack([-sine, cosine], axis=2)
    return jnp.asarray(np.concatenate([upper, lower], axis=0).astype(np.float32)).astype(jnp.bfloat16)


def row_table(rows):
    sample = jnp.arange(KR, dtype=jnp.int32)[:, None] - KR // 2
    phase = jnp.mod(rows[None, :] * sample, ROWS).astype(jnp.float32) * (2.0 * math.pi / ROWS)
    scale = jnp.where((rows >= 0) & (rows < ROWS), 1.0 / math.sqrt(KR), 0.0)[None, :]
    cosine = jnp.cos(phase) * scale
    sine = jnp.sin(phase) * scale
    upper = jnp.stack([cosine, sine], axis=1)
    lower = jnp.stack([-sine, cosine], axis=1)
    return jnp.concatenate([upper, lower], axis=0).astype(jnp.bfloat16)


def rotation(offsets, samples):
    angle = jnp.mod(offsets[:, None] * (samples[None, :] - KR // 2), ROWS).astype(jnp.float32) * (2.0 * math.pi / ROWS)
    return jnp.cos(angle), jnp.sin(angle)


def plain_body(spectra, offsets):
    own, depth = spectra.shape[:2]
    parts, strips = lax.axis_size("sub"), lax.axis_size("strip")
    wide = COLS // parts + 2
    high = ROWS // strips
    strip = lax.axis_index("strip")
    frames = own * parts
    table = column_table(spectra.shape[2] // 2, parts)
    cosine, sine = rotation(offsets, strip * depth + jnp.arange(depth, dtype=jnp.int32))
    mixed = jnp.einsum("skc,cdpn->dspnk", spectra, table, preferred_element_type=jnp.float32)
    real, imag = mixed[:, :, 0], mixed[:, :, 1]
    cosine, sine = cosine[None, :, None, :], sine[None, :, None, :]
    shifted = jnp.stack([real * cosine - imag * sine, real * sine + imag * cosine], axis=2).astype(jnp.bfloat16)
    held = lax.all_to_all(shifted, "sub", split_axis=0, concat_axis=0, tiled=True)
    held = held.reshape(frames, 2, wide, depth)
    whole = jnp.zeros((frames, 2, wide, strips, depth), jnp.bfloat16)
    for step in range(strips):
        part = held
        if step:
            part = lax.ppermute(held, "strip", [(i, (i + step) % strips) for i in range(strips)])
        source = jnp.mod(strip - step, strips)
        whole = lax.dynamic_update_slice(whole, part[:, :, :, None], (0, 0, 0, source, 0))
    wider = whole.reshape(frames, 2, wide, KR).astype(jnp.float32)
    summed = wider
    for lead in range(1, WIN):
        summed = summed + jnp.roll(wider, -lead, axis=0)
    rows = strip * high + jnp.arange(-1, high + 1, dtype=jnp.int32)
    product = jnp.einsum(
        "fpnk,pkqm->qnfm",
        summed.astype(jnp.bfloat16),
        row_table(rows).reshape(2, KR, 2, high + 2),
        preferred_element_type=jnp.float32,
    )
    log_power = jnp.log(1.0 + product[0] * product[0] + product[1] * product[1])
    total = log_power[:, :, :-2] + log_power[:, :, 1:-1] + log_power[:, :, 2:]
    filtered = (total[:-2] + total[1:-1] + total[2:]) / 9.0
    background = filtered
    for behind in range(1, BG):
        background = background + jnp.roll(filtered, behind, axis=1)
    return jnp.transpose(filtered - background / BG, (2, 0, 1))


LANES = 128
GROUP = 4
RADIX = 4
LAYERS = 4
MESH = pl.DeviceIdType.MESH


def column_planes(samples):
    phase = (np.arange(COLS)[:, None] * np.arange(samples // RADIX)[None, :] % samples) * (2.0 * math.pi / samples)
    cosine, sine = np.cos(phase) / math.sqrt(samples), -np.sin(phase) / math.sqrt(samples)
    planes = np.block([[[cosine, -sine]], [[sine, cosine]]])
    planes = planes.reshape(2, COLS // RADIX, RADIX, 2 * samples // RADIX).transpose(2, 0, 1, 3)
    planes = planes.reshape(RADIX, 2 * COLS // RADIX, 2 * samples // RADIX)
    return jnp.asarray(planes.astype(np.float32).astype(jnp.bfloat16))


def row_planes(high):
    row = np.concatenate([np.arange(high + LANES - 1), [-1]])
    used = (row <= high)[None, :]
    phase = (row[None, :] * (2 * np.arange(KR // 2)[:, None] + 1) % (2 * ROWS)) * (math.pi / ROWS)
    planes = np.concatenate([np.cos(phase) * used, -np.sin(phase) * used]) / math.sqrt(KR)
    return jnp.asarray(planes.astype(np.float32).astype(jnp.bfloat16))


def stages(upper):
    return [[2 * upper], [LAYERS - 1], [1 - upper, 2 - upper]]


def frame_weights(width, sources, rows):
    frames = 2 * sources
    weights = np.zeros((2, width, frames, rows), np.float32)
    target = np.arange(frames)

    def place(upper, at, column, frame):
        series = np.where(target == frame, 1.0, 0.0) - np.where((target - frame) % frames < BG, 1.0 / BG, 0.0)
        for near in range(max(column - 1, 0), min(column + 2, width)):
            weights[upper, near, :, at] = series

    for upper in range(2):
        at, edge_at = 0, frames * width
        for group in stages(upper):
            held = [layer * GROUP + index for layer in group for index in range(GROUP)]
            for lane in range(2):
                for source in held:
                    for spot in range(width):
                        place(upper, at, RADIX * (spot % (width // RADIX)) + spot // (width // RADIX), 2 * source + lane)
                        at += 1
            for lane in range(2):
                for source in held:
                    for side in range(2):
                        place(upper, edge_at, (-1, width)[side], 2 * source + lane)
                        edge_at += 1
    return jnp.asarray(weights.reshape(2, width * frames, rows).astype(jnp.bfloat16))


def product_of(a, b):
    return lax.dot_general(a, b, (((1,), (0,)), ((), ())), preferred_element_type=jnp.float32)


def product_t(a, b):
    return lax.dot_general(a, b, (((1,), (1,)), ((), ())), preferred_element_type=jnp.float32)


def kernel(
    parts, strips, offsets_hbm, spectra_hbm, columns_hbm, rows_hbm, weights_hbm, out_ref,
    offsets_ref, spectra, columns, rows, weights, mixed, ends, edge, main, held, lhs, boxed, level,
    load_sem, own_sem, send_sem, recv_sem, pass_sem, got_sem,
):
    me, strip = lax.axis_index("sub"), lax.axis_index("strip")
    width = COLS // parts
    depth = spectra.shape[1]
    samples = spectra.shape[2] // 2
    high = out_ref.shape[2]
    other = 1 - strip
    reach = LAYERS // 2
    layer, place = me // GROUP, lax.rem(me, GROUP)
    upper, within = layer // reach, lax.rem(layer, reach)

    def device_at(half, step, turn):
        return (half * reach + step) * GROUP + lax.rem(place + turn + GROUP, GROUP)

    close = [device_at(upper, within, turn) for turn in range(1, GROUP)]
    close += [
        device_at(upper, lax.rem(within + step, reach), turn) for step in range(1, reach) for turn in range(GROUP)
    ]
    outward = [(1 - upper) * (reach - 1) + (2 * upper - 1) * step for step in range(reach)]
    targets = [device_at(1 - upper, step, turn) for step in outward for turn in range(GROUP)]
    origins = [device_at(1 - upper, step, -turn) for step in outward for turn in range(GROUP)]

    def load(source, target, i):
        return pltpu.make_async_copy(source, target, load_sem.at[i])

    loads = [
        load(offsets_hbm, offsets_ref, 0),
        load(spectra_hbm.at[0], spectra.at[0], 1),
        load(spectra_hbm.at[1], spectra.at[1], 2),
        load(columns_hbm, columns, 3),
        load(rows_hbm, rows, 4),
        load(weights_hbm.at[upper], weights, 5),
    ]
    for copy in loads[:4]:
        copy.start()
    barrier = pltpu.get_barrier_semaphore()
    for away in range(1, parts):
        pl.semaphore_signal(barrier, inc=1, device_id=(lax.rem(me + away, parts), strip), device_id_type=MESH)
    for near in [me] + close:
        pl.semaphore_signal(barrier, inc=1, device_id=(near, other), device_id_type=MESH)

    loads[0].wait()
    lane = lax.broadcasted_iota(jnp.int32, (1, 2 * depth), 1)
    sample = strip * depth + jnp.where(lane < depth, lane, lane - depth) - KR // 2
    offset = jnp.where(lane < depth, offsets_ref[0], offsets_ref[1])
    angle = jnp.bitwise_and(offset * sample, ROWS - 1).astype(jnp.float32) * (2.0 * math.pi / ROWS)
    cosine, sine = jnp.cos(angle), jnp.sin(angle)
    edge[...] = jnp.zeros_like(edge)
    quarter = samples // RADIX
    for own in range(2):
        loads[1 + own].wait()
        re = [spectra[own, :, p * quarter : (p + 1) * quarter].astype(jnp.float32) for p in range(RADIX)]
        im = [spectra[own, :, samples + p * quarter : samples + (p + 1) * quarter].astype(jnp.float32) for p in range(RADIX)]
        even_re, even_im, gap_re, gap_im = re[0] + re[2], im[0] + im[2], re[0] - re[2], im[0] - im[2]
        odd_re, odd_im, turn_re, turn_im = re[1] + re[3], im[1] + im[3], im[1] - im[3], re[3] - re[1]
        folded = [
            (even_re + odd_re, even_im + odd_im), (gap_re + turn_re, gap_im + turn_im),
            (even_re - odd_re, even_im - odd_im), (gap_re - turn_re, gap_im - turn_im),
        ]
        for residue, pair in enumerate(folded):
            for part, value in enumerate(pair):
                mixed[residue, own * depth : (own + 1) * depth, part * quarter : (part + 1) * quarter] = value.astype(jnp.bfloat16)
    loads[3].wait()
    for copy in loads[4:]:
        copy.start()
    rank = COLS // RADIX
    slots = width // RADIX
    back = lax.broadcasted_iota(jnp.int32, (rank, depth), 1)
    back = (1 - strip) * (depth - 1 - 2 * back) + back
    for residue in range(RADIX):
        both = product_t(columns[residue], mixed[residue])
        re, im = both[:rank], both[rank:]
        for part, value in ((0, re * cosine - im * sine), (1, re * sine + im * cosine)):
            for own in range(2):
                turned = jnp.take_along_axis(value[:, own * depth : (own + 1) * depth], back, axis=1, mode="promise_in_bounds")
                into = slice(part * depth, (part + 1) * depth)
                if residue == 0:
                    ends[2 * own + 1, :, into] = turned
                if residue == RADIX - 1:
                    ends[2 * own, :, into] = turned
                main[:, own * RADIX + residue, :, into] = (
                    turned.reshape(parts, slots, depth).astype(jnp.bfloat16)
                )
    for own in range(2):
        for d in range(parts):
            if d > 0:
                edge[d, 2 * own : 2 * own + 1] = ends[2 * own, d * slots - 1 : d * slots]
            if d < parts - 1:
                edge[d, 2 * own + 1 : 2 * own + 2] = ends[2 * own + 1, (d + 1) * slots : (d + 1) * slots + 1]
    main[:, 2 * RADIX] = edge[:, :4].astype(jnp.bfloat16)

    pl.semaphore_wait(barrier, parts + len(close))

    def send(to):
        return pltpu.make_async_remote_copy(
            src_ref=main.at[to], dst_ref=held.at[strip, me], send_sem=send_sem.at[to],
            recv_sem=recv_sem.at[me], device_id=(to, strip), device_id_type=MESH,
        )

    def arrival(h, source, sem):
        return pltpu.make_async_remote_copy(
            src_ref=main.at[source], dst_ref=held.at[h, source], send_sem=send_sem.at[source],
            recv_sem=sem.at[source], device_id=(source, strip), device_id_type=MESH,
        )

    def cross(to):
        return pltpu.make_async_remote_copy(
            src_ref=main.at[to], dst_ref=held.at[strip, me], send_sem=pass_sem.at[to],
            recv_sem=got_sem.at[me], device_id=(to, other), device_id_type=MESH,
        )

    def forward(source):
        return pltpu.make_async_remote_copy(
            src_ref=held.at[strip, source], dst_ref=held.at[strip, source], send_sem=pass_sem.at[source],
            recv_sem=got_sem.at[source], device_id=(me, other), device_id_type=MESH,
        )

    for to, near in zip(targets, [me] + close):
        send(to).start()
        cross(near).start()
    for to in close:
        send(to).start()
    kept = pltpu.make_async_copy(main.at[me], held.at[strip, me], own_sem.at[0])
    kept.start()

    alternate = 1.0 - 2.0 * lax.rem(lax.broadcasted_iota(jnp.int32, (1, 1, 2 * depth), 2), 2).astype(jnp.float32)

    def sign_of(h):
        return 1.0 - strip * (1.0 + (1 - 2 * h) * alternate)

    row_at = lax.broadcasted_iota(jnp.int32, (GROUP, 8, 2 * depth), 1)

    def window(h, first, count):
        block = []
        for step in range(count + 1):
            at = lax.rem(first + step, LAYERS) * GROUP
            block.append(held[h, pl.ds(at, GROUP)].astype(jnp.float32) * sign_of(h)[None])
        whole = jnp.concatenate(block, axis=0)
        number = count * GROUP
        body = whole[:, : 2 * RADIX].reshape(number + GROUP, 2 * width, 2 * depth)
        near = whole[:, 2 * RADIX]
        near = jnp.concatenate([near, jnp.zeros_like(near)], axis=1)
        near_second = jnp.concatenate([pltpu.roll(near[i], 6, 0)[None] for i in range(number + GROUP)], axis=0)
        results = []
        for one, two in ((body[:, :width], body[:, width:]), (near, near_second)):
            pair = one + two
            double = pair[:-1] + pair[1:]
            quad = double[:number] + double[2 : number + 2]
            results.append((quad, quad - one[:number] + one[WIN // 2 : number + WIN // 2]))
        packed = []
        for frame in results[1]:
            for group in range(count):
                masked = jnp.where(row_at < 2, frame[GROUP * group : GROUP * (group + 1)], 0.0)
                total = masked[0]
                for j in range(1, GROUP):
                    total = total + pltpu.roll(masked[j], 2 * j, 0)
                packed.append(total)
        flat = [frame.reshape(number * width, 2 * depth) for frame in results[0]]
        return jnp.concatenate(flat + packed, axis=0)

    tail = lax.broadcasted_iota(jnp.int32, (1, high + LANES), 1)
    outside = ((tail == high) & (strip == strips - 1)) | ((tail == high + LANES - 1) & (strip == 0))
    inside = jnp.where(outside, 0.0, 1.0)

    facing = (2 * strip - 1).astype(jnp.float32)

    def image(mine, theirs):
        total = mine + theirs
        gap = (mine - theirs) * facing
        size = total.shape[0]
        lhs[:size, :depth] = total[:, :depth].astype(jnp.bfloat16)
        lhs[:size, depth:] = gap[:, depth:].astype(jnp.bfloat16)
        lhs[size : 2 * size, :depth] = total[:, depth:].astype(jnp.bfloat16)
        lhs[size : 2 * size, depth:] = (-gap[:, :depth]).astype(jnp.bfloat16)
        step = size // 2
        pieces = []
        for at in range(0, size, step):
            re = product_of(lhs[at : at + step], rows[...])
            im = product_of(lhs[size + at : size + at + step], rows[...])
            power = jnp.log(1.0 + re * re + im * im) * inside
            pieces.append((power + pltpu.roll(power, 1, 1) + pltpu.roll(power, high + LANES - 1, 1))[:, :high])
        return pieces

    batch = GROUP * width
    for source in origins:
        arrival(strip, source, recv_sem).wait_recv()
        forward(source).start()
    for source in close:
        arrival(strip, source, recv_sem).wait_recv()
    kept.wait()
    for source in [me] + close:
        arrival(other, source, got_sem).wait_recv()
    loads[4].wait()
    pieces = image(window(strip, 2 * upper, 1), window(other, 2 * upper, 1))
    size = 2 * batch + 2 * 8
    for i, piece in enumerate(pieces):
        boxed[0, i * (size // 2) : (i + 1) * (size // 2)] = piece
    for source in origins[:GROUP]:
        arrival(other, source, got_sem).wait_recv()
    pieces = image(window(strip, LAYERS - 1, 1), window(other, LAYERS - 1, 1))
    for i, piece in enumerate(pieces):
        boxed[1, i * (size // 2) : (i + 1) * (size // 2)] = piece
    early = boxed[:, : 2 * batch].reshape(2, 2 * GROUP, width, high)
    mean = jnp.sum(jnp.sum(early, axis=0), axis=0) * (1.0 / (4 * GROUP))
    for i in range(2):
        level[2 * batch * i : 2 * batch * (i + 1)] = (early[i] - mean[None]).reshape(2 * batch, high).astype(jnp.bfloat16)
    early_near = boxed[:, 2 * batch : size].reshape(4, 8, high)
    near_mean = jnp.sum(early_near, axis=0) * (1.0 / (4 * GROUP))
    near_mean = near_mean + pltpu.roll(near_mean, 4, 0)
    near_mean = near_mean + pltpu.roll(near_mean, 2, 0)
    top = 2 * parts * width
    level[top : top + 32] = (early_near - near_mean[None]).reshape(32, high).astype(jnp.bfloat16)
    level[top + 64 :] = jnp.zeros((level.shape[0] - top - 64, high), jnp.bfloat16)

    loads[5].wait()
    frames = 2 * parts
    step = 16
    for c in range(0, width, step):
        piece = product_of(weights[c * frames : (c + step) * frames, : 4 * batch], level[: 4 * batch])
        out_ref[c : c + step] = piece.reshape(step, frames, high)
    mine = window(strip, 1 - upper, 2)
    for source in origins[GROUP:]:
        arrival(other, source, got_sem).wait_recv()
    pieces = image(mine, window(other, 1 - upper, 2))
    late = jnp.concatenate(pieces, axis=0)
    block = late[: 4 * batch].reshape(4 * GROUP, width, high)
    level[4 * batch : 8 * batch] = (block - mean[None]).reshape(4 * batch, high).astype(jnp.bfloat16)
    late_near = late[4 * batch :].reshape(4, 8, high)
    level[top + 32 : top + 64] = (late_near - near_mean[None]).reshape(32, high).astype(jnp.bfloat16)
    for c in range(0, width, step):
        piece = product_of(weights[c * frames : (c + step) * frames, 4 * batch : 8 * batch], level[4 * batch : 8 * batch])
        piece = out_ref[c : c + step] + piece.reshape(step, frames, high)
        for edge_column in (0, width - 1):
            if c <= edge_column < c + step:
                extra = product_of(weights[edge_column * frames : (edge_column + 1) * frames, 8 * batch :], level[8 * batch :])
                row = edge_column - c
                parts_of = [piece[:row], piece[row : row + 1] + extra[None], piece[row + 1 :]]
                piece = jnp.concatenate([part for part in parts_of if part.shape[0]], axis=0)
        out_ref[c : c + step] = piece * (1.0 / 9.0)
    for to in targets + close:
        send(to).wait_send()
    for to in [me] + close:
        cross(to).wait_send()
    for source in origins:
        forward(source).wait_send()


def kernel_body(spectra, offsets):
    parts, strips = lax.axis_size("sub"), lax.axis_size("strip")
    own, depth, both = spectra.shape
    width, high = COLS // parts, ROWS // strips
    frames = own * parts
    total_rows = frames * (width + 2)
    padded = -(-total_rows // LANES) * LANES
    bf16, f32 = jnp.bfloat16, jnp.float32
    operands = (offsets, spectra, column_planes(both // 2), row_planes(high), frame_weights(width, parts, padded))
    shapes = [operand.shape for operand in operands[1:4]] + [operands[4].shape[1:]]
    half = 2 * GROUP * width + 2 * 8
    out = pl.pallas_call(
        functools.partial(kernel, parts, strips),
        out_shape=jax.ShapeDtypeStruct((width, frames, high), f32),
        in_specs=[pl.BlockSpec(memory_space=pltpu.HBM)] * 5,
        out_specs=pl.BlockSpec(memory_space=pltpu.VMEM),
        scratch_shapes=[pltpu.SMEM(offsets.shape, offsets.dtype)]
        + [pltpu.VMEM(shape, bf16) for shape in shapes]
        + [
            pltpu.VMEM((RADIX, 2 * depth, both // RADIX), bf16),
            pltpu.VMEM((4, COLS // RADIX, 2 * depth), f32),
            pltpu.VMEM((parts, 8, 2 * depth), f32),
            pltpu.VMEM((parts, 2 * RADIX + 1, width // RADIX, 2 * depth), bf16),
            pltpu.VMEM((strips, parts, 2 * RADIX + 1, width // RADIX, 2 * depth), bf16),
            pltpu.VMEM((4 * half, KR), bf16),
            pltpu.VMEM((2, half, high), f32),
            pltpu.VMEM((padded, high), bf16),
            pltpu.SemaphoreType.DMA((6,)),
            pltpu.SemaphoreType.DMA((1,)),
            pltpu.SemaphoreType.DMA((parts,)),
            pltpu.SemaphoreType.DMA((parts,)),
            pltpu.SemaphoreType.DMA((parts,)),
            pltpu.SemaphoreType.DMA((parts,)),
        ],
        compiler_params=pltpu.CompilerParams(collective_id=0, has_side_effects=True, vmem_limit_bytes=48 << 20),
        name="sar",
    )(*(pltpu.with_memory_space_constraint(operand, pltpu.HBM) for operand in operands))
    return jnp.transpose(out, (2, 0, 1))


def fits(mesh):
    parts, strips = mesh.shape["sub"], mesh.shape["strip"]
    return strips == 2 and KR // strips == LANES and COLS % parts == 0 and COLS // parts == 16 and parts == LAYERS * GROUP


def body(mesh, spectra, offsets):
    if fits(mesh) and spectra.shape[0] == 2:
        return kernel_body(spectra, offsets)
    return plain_body(spectra, offsets)


def solution(mesh):
    in_specs = (P("sub", "strip", None), P("sub"))
    out_specs = P("strip", "sub", None)
    return jax.shard_map(
        functools.partial(body, mesh), mesh=mesh, in_specs=in_specs, out_specs=out_specs, check_vma=False
    )
```

```python
import functools
import math

import jax
import jax.numpy as jnp
import numpy as np
from jax import lax
from jax.experimental import pallas as pl
from jax.experimental.pallas import tpu as pltpu
from jax.sharding import PartitionSpec as P

KR = 256
ROWS = 1024
COLS = 256
WIN = 8
BG = 16


def column_table(samples, parts):
    wide = COLS // parts + 2
    column = (np.arange(parts) * (wide - 2))[:, None] + np.arange(-1, wide - 1)[None, :]
    inside = (column >= 0) & (column < COLS)
    phase = ((np.arange(samples)[:, None, None] * column[None]) % samples) * (2.0 * math.pi / samples)
    cosine = np.where(inside, np.cos(phase), 0.0) / math.sqrt(samples)
    sine = np.where(inside, -np.sin(phase), 0.0) / math.sqrt(samples)
    upper = np.stack([cosine, sine], axis=2)
    lower = np.stack([-sine, cosine], axis=2)
    return jnp.asarray(np.concatenate([upper, lower], axis=0).astype(np.float32)).astype(jnp.bfloat16)


def row_table(rows):
    sample = jnp.arange(KR, dtype=jnp.int32)[:, None] - KR // 2
    phase = jnp.mod(rows[None, :] * sample, ROWS).astype(jnp.float32) * (2.0 * math.pi / ROWS)
    scale = jnp.where((rows >= 0) & (rows < ROWS), 1.0 / math.sqrt(KR), 0.0)[None, :]
    cosine = jnp.cos(phase) * scale
    sine = jnp.sin(phase) * scale
    upper = jnp.stack([cosine, sine], axis=1)
    lower = jnp.stack([-sine, cosine], axis=1)
    return jnp.concatenate([upper, lower], axis=0).astype(jnp.bfloat16)


def rotation(offsets, samples):
    angle = jnp.mod(offsets[:, None] * (samples[None, :] - KR // 2), ROWS).astype(jnp.float32) * (2.0 * math.pi / ROWS)
    return jnp.cos(angle), jnp.sin(angle)


def plain_body(spectra, offsets):
    own, depth = spectra.shape[:2]
    parts, strips = lax.axis_size("sub"), lax.axis_size("strip")
    wide = COLS // parts + 2
    high = ROWS // strips
    strip = lax.axis_index("strip")
    frames = own * parts
    table = column_table(spectra.shape[2] // 2, parts)
    cosine, sine = rotation(offsets, strip * depth + jnp.arange(depth, dtype=jnp.int32))
    mixed = jnp.einsum("skc,cdpn->dspnk", spectra, table, preferred_element_type=jnp.float32)
    real, imag = mixed[:, :, 0], mixed[:, :, 1]
    cosine, sine = cosine[None, :, None, :], sine[None, :, None, :]
    shifted = jnp.stack([real * cosine - imag * sine, real * sine + imag * cosine], axis=2).astype(jnp.bfloat16)
    held = lax.all_to_all(shifted, "sub", split_axis=0, concat_axis=0, tiled=True)
    held = held.reshape(frames, 2, wide, depth)
    whole = jnp.zeros((frames, 2, wide, strips, depth), jnp.bfloat16)
    for step in range(strips):
        part = held
        if step:
            part = lax.ppermute(held, "strip", [(i, (i + step) % strips) for i in range(strips)])
        source = jnp.mod(strip - step, strips)
        whole = lax.dynamic_update_slice(whole, part[:, :, :, None], (0, 0, 0, source, 0))
    wider = whole.reshape(frames, 2, wide, KR).astype(jnp.float32)
    summed = wider
    for lead in range(1, WIN):
        summed = summed + jnp.roll(wider, -lead, axis=0)
    rows = strip * high + jnp.arange(-1, high + 1, dtype=jnp.int32)
    product = jnp.einsum(
        "fpnk,pkqm->qnfm",
        summed.astype(jnp.bfloat16),
        row_table(rows).reshape(2, KR, 2, high + 2),
        preferred_element_type=jnp.float32,
    )
    log_power = jnp.log(1.0 + product[0] * product[0] + product[1] * product[1])
    total = log_power[:, :, :-2] + log_power[:, :, 1:-1] + log_power[:, :, 2:]
    filtered = (total[:-2] + total[1:-1] + total[2:]) / 9.0
    background = filtered
    for behind in range(1, BG):
        background = background + jnp.roll(filtered, behind, axis=1)
    return jnp.transpose(filtered - background / BG, (2, 0, 1))


LANES = 128
GROUP = 4
RADIX = 4
LAYERS = 4
MESH = pl.DeviceIdType.MESH


def column_planes(samples):
    phase = (np.arange(COLS)[:, None] * np.arange(samples // RADIX)[None, :] % samples) * (2.0 * math.pi / samples)
    cosine, sine = np.cos(phase) / math.sqrt(samples), -np.sin(phase) / math.sqrt(samples)
    planes = np.block([[[cosine, -sine]], [[sine, cosine]]])
    planes = planes.reshape(2, COLS // RADIX, RADIX, 2 * samples // RADIX).transpose(2, 0, 1, 3)
    planes = planes.reshape(RADIX, 2 * COLS // RADIX, 2 * samples // RADIX)
    return jnp.asarray(planes.astype(np.float32).astype(jnp.bfloat16))


def row_planes(high):
    row = np.concatenate([np.arange(high + LANES - 1), [-1]])
    used = (row <= high)[None, :]
    phase = (row[None, :] * (2 * np.arange(KR // 2)[:, None] + 1) % (2 * ROWS)) * (math.pi / ROWS)
    planes = np.concatenate([np.cos(phase) * used, -np.sin(phase) * used]) / math.sqrt(KR)
    return jnp.asarray(planes.astype(np.float32).astype(jnp.bfloat16))


def stages(upper):
    return [[2 * upper], [LAYERS - 1], [1 - upper, 2 - upper]]


def frame_weights(width, sources, rows):
    frames = 2 * sources
    weights = np.zeros((2, width, frames, rows), np.float32)
    target = np.arange(frames)

    def place(upper, at, column, frame):
        series = np.where(target == frame, 1.0, 0.0) - np.where((target - frame) % frames < BG, 1.0 / BG, 0.0)
        for near in range(max(column - 1, 0), min(column + 2, width)):
            weights[upper, near, :, at] = series

    for upper in range(2):
        at, edge_at = 0, frames * width
        for group in stages(upper):
            held = [layer * GROUP + index for layer in group for index in range(GROUP)]
            for lane in range(2):
                for source in held:
                    for spot in range(width):
                        place(upper, at, RADIX * (spot % (width // RADIX)) + spot // (width // RADIX), 2 * source + lane)
                        at += 1
            for lane in range(2):
                for source in held:
                    for side in range(2):
                        place(upper, edge_at, (-1, width)[side], 2 * source + lane)
                        edge_at += 1
    return jnp.asarray(weights.reshape(2, width * frames, rows).astype(jnp.bfloat16))


def product_of(a, b):
    return lax.dot_general(a, b, (((1,), (0,)), ((), ())), preferred_element_type=jnp.float32)


def product_t(a, b):
    return lax.dot_general(a, b, (((1,), (1,)), ((), ())), preferred_element_type=jnp.float32)


def kernel(
    parts, strips, offsets_hbm, spectra_hbm, columns_hbm, rows_hbm, weights_hbm, out_ref,
    offsets_ref, spectra, columns, rows, weights, mixed, ends, edge, main, held, lhs, boxed, level,
    load_sem, own_sem, send_sem, recv_sem, pass_sem, got_sem, entry_sem,
):
    me, strip = lax.axis_index("sub"), lax.axis_index("strip")
    width = COLS // parts
    depth = spectra.shape[1]
    samples = spectra.shape[2] // 2
    high = out_ref.shape[2]
    other = 1 - strip
    reach = LAYERS // 2
    layer, place = me // GROUP, lax.rem(me, GROUP)
    upper, within = layer // reach, lax.rem(layer, reach)

    def device_at(half, step, turn):
        return (half * reach + step) * GROUP + lax.rem(place + turn + GROUP, GROUP)

    def aside(step, shift, twist):
        row, core = lax.rem(place // 2 + shift, 2), lax.rem(place + twist, 2)
        return (upper * reach + lax.rem(within + step, reach)) * GROUP + 2 * row + core

    beside = [aside(0, 0, 1), aside(0, 1, 0), aside(0, 1, 1)]
    near = [aside(1, 0, 0), aside(1, 0, 1)]
    diagonal = [aside(1, 1, 0), aside(1, 1, 1)]
    close = beside + near + diagonal
    opening = layer == reach
    closing = layer == LAYERS - 1
    skipped = 2 * len(diagonal) * (layer // reach) * (1 - lax.rem(layer, reach))
    outward = [step for step in range(reach)]
    targets = [device_at(1 - upper, outward[step], turn) for step, turn in [(0, 0), (0, 1), (0, 2), (0, 3), (1, 0), (1, 1), (1, 2), (1, 3)]]
    waits = [(0, 0), (0, 1), (0, 2), (0, 3), (1, 0), (1, 1), (1, 2), (1, 3)]
    origins = [device_at(1 - upper, (1 - upper) + (2 * upper - 1) * step, -turn) for step, turn in waits]
    firsts = [device_at(1 - upper, 1 - upper, -turn) for turn in range(GROUP)]
    lasts = [device_at(1 - upper, upper, -turn) for turn in range(GROUP)]

    def load(source, target, i):
        return pltpu.make_async_copy(source, target, load_sem.at[i])

    loads = [
        load(offsets_hbm, offsets_ref, 0),
        load(spectra_hbm.at[0], spectra.at[0], 1),
        load(spectra_hbm.at[1], spectra.at[1], 2),
        load(columns_hbm, columns, 3),
        load(rows_hbm, rows, 4),
        load(weights_hbm.at[upper], weights, 5),
    ]
    for copy in loads[:4]:
        copy.start()
    barrier = pltpu.get_barrier_semaphore()

    def announce(to, side):
        pl.semaphore_signal(barrier, inc=1, device_id=(to, side), device_id_type=MESH)

    for to in targets + beside + near:
        announce(to, strip)
    for to in [me] + beside + near:
        announce(to, other)

    @pl.when(jnp.logical_not(closing))
    def _():
        for to in diagonal:
            announce(to, strip)
            announce(to, other)

    edge[...] = jnp.zeros_like(edge)
    quarter = samples // RADIX
    for own in range(2):
        loads[1 + own].wait()
        re = [spectra[own, :, p * quarter : (p + 1) * quarter].astype(jnp.float32) for p in range(RADIX)]
        im = [spectra[own, :, samples + p * quarter : samples + (p + 1) * quarter].astype(jnp.float32) for p in range(RADIX)]
        even_re, even_im, gap_re, gap_im = re[0] + re[2], im[0] + im[2], re[0] - re[2], im[0] - im[2]
        odd_re, odd_im, turn_re, turn_im = re[1] + re[3], im[1] + im[3], im[1] - im[3], re[3] - re[1]
        folded = [
            (even_re + odd_re, even_im + odd_im), (gap_re + turn_re, gap_im + turn_im),
            (even_re - odd_re, even_im - odd_im), (gap_re - turn_re, gap_im - turn_im),
        ]
        for residue, pair in enumerate(folded):
            for part, value in enumerate(pair):
                mixed[residue, own * depth : (own + 1) * depth, part * quarter : (part + 1) * quarter] = value.astype(jnp.bfloat16)
    loads[3].wait()
    loads[0].wait()
    lane = lax.broadcasted_iota(jnp.int32, (1, 2 * depth), 1)
    sample = strip * depth + jnp.where(lane < depth, lane, lane - depth) - KR // 2
    offset = jnp.where(lane < depth, offsets_ref[0], offsets_ref[1])
    angle = jnp.bitwise_and(offset * sample, ROWS - 1).astype(jnp.float32) * (2.0 * math.pi / ROWS)
    cosine, sine = jnp.cos(angle), jnp.sin(angle)
    for copy in loads[4:]:
        copy.start()
    rank = COLS // RADIX
    slots = width // RADIX
    back = lax.broadcasted_iota(jnp.int32, (rank, depth), 1)
    back = (1 - strip) * (depth - 1 - 2 * back) + back
    for residue in range(RADIX):
        both = product_t(columns[residue], mixed[residue])
        re, im = both[:rank], both[rank:]
        for part, value in ((0, re * cosine - im * sine), (1, re * sine + im * cosine)):
            for own in range(2):
                turned = jnp.take_along_axis(value[:, own * depth : (own + 1) * depth], back, axis=1, mode="promise_in_bounds")
                into = slice(part * depth, (part + 1) * depth)
                if residue == 0:
                    ends[2 * own + 1, :, into] = turned
                if residue == RADIX - 1:
                    ends[2 * own, :, into] = turned
                main[:, own * RADIX + residue, :, into] = (
                    turned.reshape(parts, slots, depth).astype(jnp.bfloat16)
                )
    for own in range(2):
        for d in range(parts):
            if d > 0:
                edge[d, 2 * own : 2 * own + 1] = ends[2 * own, d * slots - 1 : d * slots]
            if d < parts - 1:
                edge[d, 2 * own + 1 : 2 * own + 2] = ends[2 * own + 1, (d + 1) * slots : (d + 1) * slots + 1]
    main[:, 2 * RADIX] = edge[:, :4].astype(jnp.bfloat16)

    pl.semaphore_wait(barrier, parts + len(close) - skipped)

    def send(to):
        return pltpu.make_async_remote_copy(
            src_ref=main.at[to], dst_ref=held.at[strip, me], send_sem=send_sem.at[to],
            recv_sem=recv_sem.at[me], device_id=(to, strip), device_id_type=MESH,
        )

    def arrival(h, source, sem):
        return pltpu.make_async_remote_copy(
            src_ref=main.at[source], dst_ref=held.at[h, source], send_sem=send_sem.at[source],
            recv_sem=sem.at[source], device_id=(source, strip), device_id_type=MESH,
        )

    def cross(to):
        return pltpu.make_async_remote_copy(
            src_ref=main.at[to], dst_ref=held.at[strip, me], send_sem=pass_sem.at[to],
            recv_sem=got_sem.at[me], device_id=(to, other), device_id_type=MESH,
        )

    def forward(source):
        return pltpu.make_async_remote_copy(
            src_ref=held.at[strip, source], dst_ref=held.at[strip, source], send_sem=pass_sem.at[source],
            recv_sem=got_sem.at[source], device_id=(me, other), device_id_type=MESH,
        )

    for index, to in enumerate(targets):
        send(to).start()
        if index < len(close) - 1:
            cross(([me] + beside + near)[index]).start()
    for to in beside + near:
        send(to).start()

    def send_diagonal():
        for to in diagonal:
            send(to).start()
            cross(to).start()

    pl.when(jnp.logical_not(opening))(send_diagonal)

    @pl.when(closing)
    def _():
        for to in diagonal:
            pl.semaphore_signal(entry_sem, inc=1, device_id=(to, strip), device_id_type=MESH)
            pl.semaphore_signal(entry_sem, inc=1, device_id=(to, other), device_id_type=MESH)

    kept = pltpu.make_async_copy(main.at[me], held.at[strip, me], own_sem.at[0])
    kept.start()

    @pl.when(opening)
    def _():
        pl.semaphore_wait(entry_sem, 2 * len(diagonal))
        send_diagonal()


    alternate = 1.0 - 2.0 * lax.rem(lax.broadcasted_iota(jnp.int32, (1, 1, 2 * depth), 2), 2).astype(jnp.float32)

    def sign_of(h):
        return 1.0 - strip * (1.0 + (1 - 2 * h) * alternate)

    row_at = lax.broadcasted_iota(jnp.int32, (GROUP, 8, 2 * depth), 1)

    def window(h, first, count):
        block = []
        for step in range(count + 1):
            at = lax.rem(first + step, LAYERS) * GROUP
            block.append(held[h, pl.ds(at, GROUP)].astype(jnp.float32) * sign_of(h)[None])
        whole = jnp.concatenate(block, axis=0)
        number = count * GROUP
        body = whole[:, : 2 * RADIX].reshape(number + GROUP, 2 * width, 2 * depth)
        near = whole[:, 2 * RADIX]
        near = jnp.concatenate([near, jnp.zeros_like(near)], axis=1)
        near_second = jnp.concatenate([pltpu.roll(near[i], 6, 0)[None] for i in range(number + GROUP)], axis=0)
        results = []
        for one, two in ((body[:, :width], body[:, width:]), (near, near_second)):
            pair = one + two
            double = pair[:-1] + pair[1:]
            quad = double[:number] + double[2 : number + 2]
            results.append((quad, quad - one[:number] + one[WIN // 2 : number + WIN // 2]))
        packed = []
        for frame in results[1]:
            for group in range(count):
                masked = jnp.where(row_at < 2, frame[GROUP * group : GROUP * (group + 1)], 0.0)
                total = masked[0]
                for j in range(1, GROUP):
                    total = total + pltpu.roll(masked[j], 2 * j, 0)
                packed.append(total)
        flat = [frame.reshape(number * width, 2 * depth) for frame in results[0]]
        return jnp.concatenate(flat + packed, axis=0)

    tail = lax.broadcasted_iota(jnp.int32, (1, high + LANES), 1)
    outside = ((tail == high) & (strip == strips - 1)) | ((tail == high + LANES - 1) & (strip == 0))
    inside = jnp.where(outside, 0.0, 1.0)

    facing = (2 * strip - 1).astype(jnp.float32)

    def image(mine, theirs):
        total = mine + theirs
        gap = (mine - theirs) * facing
        size = total.shape[0]
        lhs[:size, :depth] = total[:, :depth].astype(jnp.bfloat16)
        lhs[:size, depth:] = gap[:, depth:].astype(jnp.bfloat16)
        lhs[size : 2 * size, :depth] = total[:, depth:].astype(jnp.bfloat16)
        lhs[size : 2 * size, depth:] = (-gap[:, :depth]).astype(jnp.bfloat16)
        step = size // 2
        pieces = []
        for at in range(0, size, step):
            re = product_of(lhs[at : at + step], rows[...])
            im = product_of(lhs[size + at : size + at + step], rows[...])
            power = jnp.log(1.0 + re * re + im * im) * inside
            pieces.append((power + pltpu.roll(power, 1, 1) + pltpu.roll(power, high + LANES - 1, 1))[:, :high])
        return pieces

    batch = GROUP * width
    for source in origins:
        arrival(strip, source, recv_sem).wait_recv()
        forward(source).start()
    for source in close:
        arrival(strip, source, recv_sem).wait_recv()
    kept.wait()
    for source in [me] + close:
        arrival(other, source, got_sem).wait_recv()
    loads[4].wait()
    pieces = image(window(strip, 2 * upper, 1), window(other, 2 * upper, 1))
    size = 2 * batch + 2 * 8
    for i, piece in enumerate(pieces):
        boxed[0, i * (size // 2) : (i + 1) * (size // 2)] = piece
    for source in firsts:
        arrival(other, source, got_sem).wait_recv()
    pieces = image(window(strip, LAYERS - 1, 1), window(other, LAYERS - 1, 1))
    for i, piece in enumerate(pieces):
        boxed[1, i * (size // 2) : (i + 1) * (size // 2)] = piece
    early = boxed[:, : 2 * batch].reshape(2, 2 * GROUP, width, high)
    mean = jnp.sum(jnp.sum(early, axis=0), axis=0) * (1.0 / (4 * GROUP))
    for i in range(2):
        level[2 * batch * i : 2 * batch * (i + 1)] = (early[i] - mean[None]).reshape(2 * batch, high).astype(jnp.bfloat16)
    early_near = boxed[:, 2 * batch : size].reshape(4, 8, high)
    near_mean = jnp.sum(early_near, axis=0) * (1.0 / (4 * GROUP))
    near_mean = near_mean + pltpu.roll(near_mean, 4, 0)
    near_mean = near_mean + pltpu.roll(near_mean, 2, 0)
    top = 2 * parts * width
    level[top : top + 32] = (early_near - near_mean[None]).reshape(32, high).astype(jnp.bfloat16)
    level[top + 64 :] = jnp.zeros((level.shape[0] - top - 64, high), jnp.bfloat16)

    loads[5].wait()
    frames = 2 * parts
    step = 16
    for c in range(0, width, step):
        piece = product_of(weights[c * frames : (c + step) * frames, : 4 * batch], level[: 4 * batch])
        out_ref[c : c + step] = piece.reshape(step, frames, high)
    mine = window(strip, 1 - upper, 2)
    for source in lasts:
        arrival(other, source, got_sem).wait_recv()
    pieces = image(mine, window(other, 1 - upper, 2))
    late = jnp.concatenate(pieces, axis=0)
    block = late[: 4 * batch].reshape(4 * GROUP, width, high)
    level[4 * batch : 8 * batch] = (block - mean[None]).reshape(4 * batch, high).astype(jnp.bfloat16)
    late_near = late[4 * batch :].reshape(4, 8, high)
    level[top + 32 : top + 64] = (late_near - near_mean[None]).reshape(32, high).astype(jnp.bfloat16)
    for c in range(0, width, step):
        piece = product_of(weights[c * frames : (c + step) * frames, 4 * batch : 8 * batch], level[4 * batch : 8 * batch])
        piece = out_ref[c : c + step] + piece.reshape(step, frames, high)
        for edge_column in (0, width - 1):
            if c <= edge_column < c + step:
                extra = product_of(weights[edge_column * frames : (edge_column + 1) * frames, 8 * batch :], level[8 * batch :])
                row = edge_column - c
                parts_of = [piece[:row], piece[row : row + 1] + extra[None], piece[row + 1 :]]
                piece = jnp.concatenate([part for part in parts_of if part.shape[0]], axis=0)
        out_ref[c : c + step] = piece * (1.0 / 9.0)
    for to in targets + close:
        send(to).wait_send()
    for to in [me] + close:
        cross(to).wait_send()
    for source in origins:
        forward(source).wait_send()


def kernel_body(spectra, offsets):
    parts, strips = lax.axis_size("sub"), lax.axis_size("strip")
    own, depth, both = spectra.shape
    width, high = COLS // parts, ROWS // strips
    frames = own * parts
    total_rows = frames * (width + 2)
    padded = -(-total_rows // LANES) * LANES
    bf16, f32 = jnp.bfloat16, jnp.float32
    operands = (offsets, spectra, column_planes(both // 2), row_planes(high), frame_weights(width, parts, padded))
    shapes = [operand.shape for operand in operands[1:4]] + [operands[4].shape[1:]]
    half = 2 * GROUP * width + 2 * 8
    out = pl.pallas_call(
        functools.partial(kernel, parts, strips),
        out_shape=jax.ShapeDtypeStruct((width, frames, high), f32),
        in_specs=[pl.BlockSpec(memory_space=pltpu.HBM)] * 5,
        out_specs=pl.BlockSpec(memory_space=pltpu.VMEM),
        scratch_shapes=[pltpu.SMEM(offsets.shape, offsets.dtype)]
        + [pltpu.VMEM(shape, bf16) for shape in shapes]
        + [
            pltpu.VMEM((RADIX, 2 * depth, both // RADIX), bf16),
            pltpu.VMEM((4, COLS // RADIX, 2 * depth), f32),
            pltpu.VMEM((parts, 8, 2 * depth), f32),
            pltpu.VMEM((parts, 2 * RADIX + 1, width // RADIX, 2 * depth), bf16),
            pltpu.VMEM((strips, parts, 2 * RADIX + 1, width // RADIX, 2 * depth), bf16),
            pltpu.VMEM((4 * half, KR), bf16),
            pltpu.VMEM((2, half, high), f32),
            pltpu.VMEM((padded, high), bf16),
            pltpu.SemaphoreType.DMA((6,)),
            pltpu.SemaphoreType.DMA((1,)),
            pltpu.SemaphoreType.DMA((parts,)),
            pltpu.SemaphoreType.DMA((parts,)),
            pltpu.SemaphoreType.DMA((parts,)),
            pltpu.SemaphoreType.DMA((parts,)),
            pltpu.SemaphoreType.REGULAR,
        ],
        compiler_params=pltpu.CompilerParams(collective_id=0, has_side_effects=True, vmem_limit_bytes=48 << 20),
        name="sar",
    )(*(pltpu.with_memory_space_constraint(operand, pltpu.HBM) for operand in operands))
    return jnp.transpose(out, (2, 0, 1))


def fits(mesh):
    parts, strips = mesh.shape["sub"], mesh.shape["strip"]
    return strips == 2 and KR // strips == LANES and COLS % parts == 0 and COLS // parts == 16 and parts == LAYERS * GROUP


def body(mesh, spectra, offsets):
    if fits(mesh) and spectra.shape[0] == 2:
        return kernel_body(spectra, offsets)
    return plain_body(spectra, offsets)


def solution(mesh):
    in_specs = (P("sub", "strip", None), P("sub"))
    out_specs = P("strip", "sub", None)
    return jax.shard_map(
        functools.partial(body, mesh), mesh=mesh, in_specs=in_specs, out_specs=out_specs, check_vma=False
    )
```

```python
import functools
import math

import jax
import jax.numpy as jnp
import numpy as np
from jax import lax
from jax.experimental import pallas as pl
from jax.experimental.pallas import tpu as pltpu
from jax.sharding import PartitionSpec as P

KR = 256
ROWS = 1024
COLS = 256
WIN = 8
BG = 16


def column_table(samples, parts):
    wide = COLS // parts + 2
    column = (np.arange(parts) * (wide - 2))[:, None] + np.arange(-1, wide - 1)[None, :]
    inside = (column >= 0) & (column < COLS)
    phase = ((np.arange(samples)[:, None, None] * column[None]) % samples) * (2.0 * math.pi / samples)
    cosine = np.where(inside, np.cos(phase), 0.0) / math.sqrt(samples)
    sine = np.where(inside, -np.sin(phase), 0.0) / math.sqrt(samples)
    upper = np.stack([cosine, sine], axis=2)
    lower = np.stack([-sine, cosine], axis=2)
    return jnp.asarray(np.concatenate([upper, lower], axis=0).astype(np.float32)).astype(jnp.bfloat16)


def row_table(rows):
    sample = jnp.arange(KR, dtype=jnp.int32)[:, None] - KR // 2
    phase = jnp.mod(rows[None, :] * sample, ROWS).astype(jnp.float32) * (2.0 * math.pi / ROWS)
    scale = jnp.where((rows >= 0) & (rows < ROWS), 1.0 / math.sqrt(KR), 0.0)[None, :]
    cosine = jnp.cos(phase) * scale
    sine = jnp.sin(phase) * scale
    upper = jnp.stack([cosine, sine], axis=1)
    lower = jnp.stack([-sine, cosine], axis=1)
    return jnp.concatenate([upper, lower], axis=0).astype(jnp.bfloat16)


def rotation(offsets, samples):
    angle = jnp.mod(offsets[:, None] * (samples[None, :] - KR // 2), ROWS).astype(jnp.float32) * (2.0 * math.pi / ROWS)
    return jnp.cos(angle), jnp.sin(angle)


def plain_body(spectra, offsets):
    own, depth = spectra.shape[:2]
    parts, strips = lax.axis_size("sub"), lax.axis_size("strip")
    wide = COLS // parts + 2
    high = ROWS // strips
    strip = lax.axis_index("strip")
    frames = own * parts
    table = column_table(spectra.shape[2] // 2, parts)
    cosine, sine = rotation(offsets, strip * depth + jnp.arange(depth, dtype=jnp.int32))
    mixed = jnp.einsum("skc,cdpn->dspnk", spectra, table, preferred_element_type=jnp.float32)
    real, imag = mixed[:, :, 0], mixed[:, :, 1]
    cosine, sine = cosine[None, :, None, :], sine[None, :, None, :]
    shifted = jnp.stack([real * cosine - imag * sine, real * sine + imag * cosine], axis=2).astype(jnp.bfloat16)
    held = lax.all_to_all(shifted, "sub", split_axis=0, concat_axis=0, tiled=True)
    held = held.reshape(frames, 2, wide, depth)
    whole = jnp.zeros((frames, 2, wide, strips, depth), jnp.bfloat16)
    for step in range(strips):
        part = held
        if step:
            part = lax.ppermute(held, "strip", [(i, (i + step) % strips) for i in range(strips)])
        source = jnp.mod(strip - step, strips)
        whole = lax.dynamic_update_slice(whole, part[:, :, :, None], (0, 0, 0, source, 0))
    wider = whole.reshape(frames, 2, wide, KR).astype(jnp.float32)
    summed = wider
    for lead in range(1, WIN):
        summed = summed + jnp.roll(wider, -lead, axis=0)
    rows = strip * high + jnp.arange(-1, high + 1, dtype=jnp.int32)
    product = jnp.einsum(
        "fpnk,pkqm->qnfm",
        summed.astype(jnp.bfloat16),
        row_table(rows).reshape(2, KR, 2, high + 2),
        preferred_element_type=jnp.float32,
    )
    log_power = jnp.log(1.0 + product[0] * product[0] + product[1] * product[1])
    total = log_power[:, :, :-2] + log_power[:, :, 1:-1] + log_power[:, :, 2:]
    filtered = (total[:-2] + total[1:-1] + total[2:]) / 9.0
    background = filtered
    for behind in range(1, BG):
        background = background + jnp.roll(filtered, behind, axis=1)
    return jnp.transpose(filtered - background / BG, (2, 0, 1))


LANES = 128
GROUP = 4
RADIX = 4
LAYERS = 4
MESH = pl.DeviceIdType.MESH


def column_planes(samples):
    phase = (np.arange(COLS)[:, None] * np.arange(samples // RADIX)[None, :] % samples) * (2.0 * math.pi / samples)
    cosine, sine = np.cos(phase) / math.sqrt(samples), -np.sin(phase) / math.sqrt(samples)
    planes = np.block([[[cosine, -sine]], [[sine, cosine]]])
    planes = planes.reshape(2, COLS // RADIX, RADIX, 2 * samples // RADIX).transpose(2, 0, 1, 3)
    planes = planes.reshape(RADIX, 2 * COLS // RADIX, 2 * samples // RADIX)
    return jnp.asarray(planes.astype(np.float32).astype(jnp.bfloat16))


def row_planes(high):
    row = np.concatenate([np.arange(high + LANES - 1), [-1]])
    used = (row <= high)[None, :]
    phase = (row[None, :] * (2 * np.arange(KR // 2)[:, None] + 1) % (2 * ROWS)) * (math.pi / ROWS)
    planes = np.concatenate([np.cos(phase) * used, -np.sin(phase) * used]) / math.sqrt(KR)
    return jnp.asarray(planes.astype(np.float32).astype(jnp.bfloat16))


def stages(upper):
    return [[2 * upper], [LAYERS - 1], [1 - upper, 2 - upper]]


def frame_weights(width, sources, rows):
    frames = 2 * sources
    weights = np.zeros((2, width, frames, rows), np.float32)
    target = np.arange(frames)

    def place(upper, at, column, frame):
        series = np.where(target == frame, 1.0, 0.0) - np.where((target - frame) % frames < BG, 1.0 / BG, 0.0)
        for near in range(max(column - 1, 0), min(column + 2, width)):
            weights[upper, near, :, at] = series

    for upper in range(2):
        at, edge_at = 0, frames * width
        for group in stages(upper):
            held = [layer * GROUP + index for layer in group for index in range(GROUP)]
            for lane in range(2):
                for source in held:
                    for spot in range(width):
                        place(upper, at, RADIX * (spot % (width // RADIX)) + spot // (width // RADIX), 2 * source + lane)
                        at += 1
            for lane in range(2):
                for source in held:
                    for side in range(2):
                        place(upper, edge_at, (-1, width)[side], 2 * source + lane)
                        edge_at += 1
    return jnp.asarray(weights.reshape(2, width * frames, rows).astype(jnp.bfloat16))


def product_of(a, b):
    return lax.dot_general(a, b, (((1,), (0,)), ((), ())), preferred_element_type=jnp.float32)


def product_t(a, b):
    return lax.dot_general(a, b, (((1,), (1,)), ((), ())), preferred_element_type=jnp.float32)


def kernel(
    parts, strips, offsets_hbm, spectra_hbm, columns_hbm, rows_hbm, weights_hbm, out_ref,
    offsets_ref, spectra, columns, rows, weights, mixed, ends, edge, main, held, lhs, boxed, level,
    load_sem, own_sem, send_sem, recv_sem, got_sem, entry_sem,
):
    me, strip = lax.axis_index("sub"), lax.axis_index("strip")
    width = COLS // parts
    depth = spectra.shape[1]
    samples = spectra.shape[2] // 2
    high = out_ref.shape[2]
    other = 1 - strip
    reach = LAYERS // 2
    layer, place = me // GROUP, lax.rem(me, GROUP)
    upper, within = layer // reach, lax.rem(layer, reach)

    def device_at(half, step, turn):
        return (half * reach + step) * GROUP + lax.rem(place + turn + GROUP, GROUP)

    def aside(step, shift, twist):
        row, core = lax.rem(place // 2 + shift, 2), lax.rem(place + twist, 2)
        return (upper * reach + lax.rem(within + step, reach)) * GROUP + 2 * row + core

    beside = [aside(0, 0, 1), aside(0, 1, 0), aside(0, 1, 1)]
    near = [aside(1, 0, 0), aside(1, 0, 1)]
    diagonal = [aside(1, 1, 0), aside(1, 1, 1)]
    close = beside + near + diagonal
    opening = layer == reach
    closing = layer == LAYERS - 1
    skipped = 2 * len(diagonal) * (layer // reach) * (1 - lax.rem(layer, reach))
    outward = [step for step in range(reach)]
    targets = [device_at(1 - upper, outward[step], turn) for step, turn in [(0, 0), (0, 1), (0, 2), (0, 3), (1, 0), (1, 1), (1, 2), (1, 3)]]
    waits = [(0, 0), (0, 1), (0, 2), (0, 3), (1, 0), (1, 1), (1, 2), (1, 3)]
    origins = [device_at(1 - upper, (1 - upper) + (2 * upper - 1) * step, -turn) for step, turn in waits]

    def load(source, target, i):
        return pltpu.make_async_copy(source, target, load_sem.at[i])

    loads = [
        load(offsets_hbm, offsets_ref, 0),
        load(spectra_hbm, spectra, 1),
        load(columns_hbm, columns, 2),
        load(rows_hbm, rows, 3),
        load(weights_hbm.at[upper], weights, 4),
    ]
    for copy in loads[:3]:
        copy.start()
    barrier = pltpu.get_barrier_semaphore()

    def announce(to, side):
        pl.semaphore_signal(barrier, inc=1, device_id=(to, side), device_id_type=MESH)

    for to in targets + beside + near:
        announce(to, strip)
    for to in [me] + beside + near:
        announce(to, other)

    @pl.when(jnp.logical_not(closing))
    def _():
        for to in diagonal:
            announce(to, strip)
            announce(to, other)

    edge[...] = jnp.zeros_like(edge)
    quarter = samples // RADIX
    loads[1].wait()
    for own in range(2):
        re = [spectra[own, :, p * quarter : (p + 1) * quarter].astype(jnp.float32) for p in range(RADIX)]
        im = [spectra[own, :, samples + p * quarter : samples + (p + 1) * quarter].astype(jnp.float32) for p in range(RADIX)]
        even_re, even_im, gap_re, gap_im = re[0] + re[2], im[0] + im[2], re[0] - re[2], im[0] - im[2]
        odd_re, odd_im, turn_re, turn_im = re[1] + re[3], im[1] + im[3], im[1] - im[3], re[3] - re[1]
        folded = [
            (even_re + odd_re, even_im + odd_im), (gap_re + turn_re, gap_im + turn_im),
            (even_re - odd_re, even_im - odd_im), (gap_re - turn_re, gap_im - turn_im),
        ]
        for residue, pair in enumerate(folded):
            for part, value in enumerate(pair):
                mixed[residue, own * depth : (own + 1) * depth, part * quarter : (part + 1) * quarter] = value.astype(jnp.bfloat16)
    loads[2].wait()
    loads[0].wait()
    lane = lax.broadcasted_iota(jnp.int32, (1, 2 * depth), 1)
    sample = strip * depth + jnp.where(lane < depth, lane, lane - depth) - KR // 2
    offset = jnp.where(lane < depth, offsets_ref[0], offsets_ref[1])
    angle = jnp.bitwise_and(offset * sample, ROWS - 1).astype(jnp.float32) * (2.0 * math.pi / ROWS)
    cosine, sine = jnp.cos(angle), jnp.sin(angle)
    for copy in loads[3:]:
        copy.start()
    rank = COLS // RADIX
    slots = width // RADIX
    back = lax.broadcasted_iota(jnp.int32, (rank, depth), 1)
    back = (1 - strip) * (depth - 1 - 2 * back) + back
    for residue in range(RADIX):
        both = product_t(columns[residue], mixed[residue])
        re, im = both[:rank], both[rank:]
        for part, value in ((0, re * cosine - im * sine), (1, re * sine + im * cosine)):
            for own in range(2):
                turned = jnp.take_along_axis(value[:, own * depth : (own + 1) * depth], back, axis=1, mode="promise_in_bounds")
                into = slice(part * depth, (part + 1) * depth)
                if residue == 0:
                    ends[2 * own + 1, :, into] = turned
                if residue == RADIX - 1:
                    ends[2 * own, :, into] = turned
                main[:, own * RADIX + residue, :, into] = (
                    turned.reshape(parts, slots, depth).astype(jnp.bfloat16)
                )
    for own in range(2):
        for d in range(parts):
            if d > 0:
                edge[d, 2 * own : 2 * own + 1] = ends[2 * own, d * slots - 1 : d * slots]
            if d < parts - 1:
                edge[d, 2 * own + 1 : 2 * own + 2] = ends[2 * own + 1, (d + 1) * slots : (d + 1) * slots + 1]
    main[:, 2 * RADIX] = edge[:, :4].astype(jnp.bfloat16)

    pl.semaphore_wait(barrier, parts + len(close) - skipped)

    def remote(source, h, to, side, sent, landed):
        return pltpu.make_async_remote_copy(
            src_ref=source, dst_ref=held.at[strip, h], send_sem=sent, recv_sem=landed,
            device_id=(to, side), device_id_type=MESH,
        )

    def send(to):
        return remote(main.at[to], me, to, strip, send_sem.at[0], recv_sem.at[parts // 2])

    def send_far(to):
        return remote(main.at[to], me, to, strip, send_sem.at[0], recv_sem.at[lax.rem(me, parts // 2)])

    def cross(to):
        return remote(main.at[to], me, to, other, send_sem.at[1], got_sem.at[0])

    def forward(source, group):
        return remote(held.at[strip, source], source, me, other, send_sem.at[1], got_sem.at[1 + group])

    def far_arrival(source):
        sem = recv_sem.at[lax.rem(source, parts // 2)]
        return pltpu.make_async_copy(main.at[source], held.at[strip, source], sem)

    def together(h, number, sem):
        return pltpu.make_async_copy(main.at[pl.ds(0, number)], held.at[h, pl.ds(0, number)], sem)

    for index, to in enumerate(targets):
        send_far(to).start()
        if index < len(close) - 1:
            cross(([me] + beside + near)[index]).start()
    for to in beside + near:
        send(to).start()

    def send_diagonal():
        for to in diagonal:
            send(to).start()
            cross(to).start()

    pl.when(jnp.logical_not(opening))(send_diagonal)

    @pl.when(closing)
    def _():
        for to in diagonal:
            pl.semaphore_signal(entry_sem, inc=1, device_id=(to, strip), device_id_type=MESH)
            pl.semaphore_signal(entry_sem, inc=1, device_id=(to, other), device_id_type=MESH)

    kept = pltpu.make_async_copy(main.at[me], held.at[strip, me], own_sem.at[0])
    kept.start()

    @pl.when(opening)
    def _():
        pl.semaphore_wait(entry_sem, 2 * len(diagonal))
        send_diagonal()


    alternate = 1.0 - 2.0 * lax.rem(lax.broadcasted_iota(jnp.int32, (1, 1, 2 * depth), 2), 2).astype(jnp.float32)

    def sign_of(h):
        return 1.0 - strip * (1.0 + (1 - 2 * h) * alternate)

    row_at = lax.broadcasted_iota(jnp.int32, (GROUP, 8, 2 * depth), 1)

    def window(h, first, count):
        block = []
        for step in range(count + 1):
            at = lax.rem(first + step, LAYERS) * GROUP
            block.append(held[h, pl.ds(at, GROUP)].astype(jnp.float32) * sign_of(h)[None])
        whole = jnp.concatenate(block, axis=0)
        number = count * GROUP
        body = whole[:, : 2 * RADIX].reshape(number + GROUP, 2 * width, 2 * depth)
        near = whole[:, 2 * RADIX]
        near = jnp.concatenate([near, jnp.zeros_like(near)], axis=1)
        near_second = jnp.concatenate([pltpu.roll(near[i], 6, 0)[None] for i in range(number + GROUP)], axis=0)
        results = []
        for one, two in ((body[:, :width], body[:, width:]), (near, near_second)):
            pair = one + two
            double = pair[:-1] + pair[1:]
            quad = double[:number] + double[2 : number + 2]
            results.append((quad, quad - one[:number] + one[WIN // 2 : number + WIN // 2]))
        packed = []
        for frame in results[1]:
            for group in range(count):
                masked = jnp.where(row_at < 2, frame[GROUP * group : GROUP * (group + 1)], 0.0)
                total = masked[0]
                for j in range(1, GROUP):
                    total = total + pltpu.roll(masked[j], 2 * j, 0)
                packed.append(total)
        flat = [frame.reshape(number * width, 2 * depth) for frame in results[0]]
        return jnp.concatenate(flat + packed, axis=0)

    tail = lax.broadcasted_iota(jnp.int32, (1, high + LANES), 1)
    outside = ((tail == high) & (strip == strips - 1)) | ((tail == high + LANES - 1) & (strip == 0))
    inside = jnp.where(outside, 0.0, 1.0)

    facing = (2 * strip - 1).astype(jnp.float32)

    def image(mine, theirs):
        total = mine + theirs
        gap = (mine - theirs) * facing
        size = total.shape[0]
        lhs[:size, :depth] = total[:, :depth].astype(jnp.bfloat16)
        lhs[:size, depth:] = gap[:, depth:].astype(jnp.bfloat16)
        lhs[size : 2 * size, :depth] = total[:, depth:].astype(jnp.bfloat16)
        lhs[size : 2 * size, depth:] = (-gap[:, :depth]).astype(jnp.bfloat16)
        step = size // 2
        pieces = []
        for at in range(0, size, step):
            re = product_of(lhs[at : at + step], rows[...])
            im = product_of(lhs[size + at : size + at + step], rows[...])
            power = jnp.log(1.0 + re * re + im * im) * inside
            pieces.append((power + pltpu.roll(power, 1, 1) + pltpu.roll(power, high + LANES - 1, 1))[:, :high])
        return pieces

    batch = GROUP * width
    for index, source in enumerate(origins):
        far_arrival(source).wait()
        forward(source, index // GROUP).start()
    together(strip, len(close), recv_sem.at[parts // 2]).wait()
    kept.wait()
    together(other, parts // 2, got_sem.at[0]).wait()
    loads[3].wait()
    pieces = image(window(strip, 2 * upper, 1), window(other, 2 * upper, 1))
    size = 2 * batch + 2 * 8
    for i, piece in enumerate(pieces):
        boxed[0, i * (size // 2) : (i + 1) * (size // 2)] = piece
    together(other, GROUP, got_sem.at[1]).wait()
    pieces = image(window(strip, LAYERS - 1, 1), window(other, LAYERS - 1, 1))
    for i, piece in enumerate(pieces):
        boxed[1, i * (size // 2) : (i + 1) * (size // 2)] = piece
    early = boxed[:, : 2 * batch].reshape(2, 2 * GROUP, width, high)
    mean = jnp.sum(jnp.sum(early, axis=0), axis=0) * (1.0 / (4 * GROUP))
    for i in range(2):
        level[2 * batch * i : 2 * batch * (i + 1)] = (early[i] - mean[None]).reshape(2 * batch, high).astype(jnp.bfloat16)
    early_near = boxed[:, 2 * batch : size].reshape(4, 8, high)
    near_mean = jnp.sum(early_near, axis=0) * (1.0 / (4 * GROUP))
    near_mean = near_mean + pltpu.roll(near_mean, 4, 0)
    near_mean = near_mean + pltpu.roll(near_mean, 2, 0)
    top = 2 * parts * width
    level[top : top + 32] = (early_near - near_mean[None]).reshape(32, high).astype(jnp.bfloat16)
    level[top + 64 :] = jnp.zeros((level.shape[0] - top - 64, high), jnp.bfloat16)

    loads[4].wait()
    frames = 2 * parts
    step = 16
    for c in range(0, width, step):
        piece = product_of(weights[c * frames : (c + step) * frames, : 4 * batch], level[: 4 * batch])
        out_ref[c : c + step] = piece.reshape(step, frames, high)
    mine = window(strip, 1 - upper, 2)
    together(other, GROUP, got_sem.at[2]).wait()
    pieces = image(mine, window(other, 1 - upper, 2))
    late = jnp.concatenate(pieces, axis=0)
    block = late[: 4 * batch].reshape(4 * GROUP, width, high)
    level[4 * batch : 8 * batch] = (block - mean[None]).reshape(4 * batch, high).astype(jnp.bfloat16)
    late_near = late[4 * batch :].reshape(4, 8, high)
    level[top + 32 : top + 64] = (late_near - near_mean[None]).reshape(32, high).astype(jnp.bfloat16)
    for c in range(0, width, step):
        piece = product_of(weights[c * frames : (c + step) * frames, 4 * batch : 8 * batch], level[4 * batch : 8 * batch])
        piece = out_ref[c : c + step] + piece.reshape(step, frames, high)
        for edge_column in (0, width - 1):
            if c <= edge_column < c + step:
                extra = product_of(weights[edge_column * frames : (edge_column + 1) * frames, 8 * batch :], level[8 * batch :])
                row = edge_column - c
                parts_of = [piece[:row], piece[row : row + 1] + extra[None], piece[row + 1 :]]
                piece = jnp.concatenate([part for part in parts_of if part.shape[0]], axis=0)
        out_ref[c : c + step] = piece * (1.0 / 9.0)
    together(strip, parts - 1, send_sem.at[0]).wait()
    together(strip, parts, send_sem.at[1]).wait()


def kernel_body(spectra, offsets):
    parts, strips = lax.axis_size("sub"), lax.axis_size("strip")
    own, depth, both = spectra.shape
    width, high = COLS // parts, ROWS // strips
    frames = own * parts
    total_rows = frames * (width + 2)
    padded = -(-total_rows // LANES) * LANES
    bf16, f32 = jnp.bfloat16, jnp.float32
    operands = (offsets, spectra, column_planes(both // 2), row_planes(high), frame_weights(width, parts, padded))
    shapes = [operand.shape for operand in operands[1:4]] + [operands[4].shape[1:]]
    half = 2 * GROUP * width + 2 * 8
    out = pl.pallas_call(
        functools.partial(kernel, parts, strips),
        out_shape=jax.ShapeDtypeStruct((width, frames, high), f32),
        in_specs=[pl.BlockSpec(memory_space=pltpu.HBM)] * 5,
        out_specs=pl.BlockSpec(memory_space=pltpu.VMEM),
        scratch_shapes=[pltpu.SMEM(offsets.shape, offsets.dtype)]
        + [pltpu.VMEM(shape, bf16) for shape in shapes]
        + [
            pltpu.VMEM((RADIX, 2 * depth, both // RADIX), bf16),
            pltpu.VMEM((4, COLS // RADIX, 2 * depth), f32),
            pltpu.VMEM((parts, 8, 2 * depth), f32),
            pltpu.VMEM((parts, 2 * RADIX + 1, width // RADIX, 2 * depth), bf16),
            pltpu.VMEM((strips, parts, 2 * RADIX + 1, width // RADIX, 2 * depth), bf16),
            pltpu.VMEM((4 * half, KR), bf16),
            pltpu.VMEM((2, half, high), f32),
            pltpu.VMEM((padded, high), bf16),
            pltpu.SemaphoreType.DMA((5,)),
            pltpu.SemaphoreType.DMA((1,)),
            pltpu.SemaphoreType.DMA((2,)),
            pltpu.SemaphoreType.DMA((parts // 2 + 1,)),
            pltpu.SemaphoreType.DMA((3,)),
            pltpu.SemaphoreType.REGULAR,
        ],
        compiler_params=pltpu.CompilerParams(collective_id=0, has_side_effects=True, vmem_limit_bytes=48 << 20),
        name="sar",
    )(*(pltpu.with_memory_space_constraint(operand, pltpu.HBM) for operand in operands))
    return jnp.transpose(out, (2, 0, 1))


def fits(mesh):
    parts, strips = mesh.shape["sub"], mesh.shape["strip"]
    return strips == 2 and KR // strips == LANES and COLS % parts == 0 and COLS // parts == 16 and parts == LAYERS * GROUP


def body(mesh, spectra, offsets):
    if fits(mesh) and spectra.shape[0] == 2:
        return kernel_body(spectra, offsets)
    return plain_body(spectra, offsets)


def solution(mesh):
    in_specs = (P("sub", "strip", None), P("sub"))
    out_specs = P("strip", "sub", None)
    return jax.shard_map(
        functools.partial(body, mesh), mesh=mesh, in_specs=in_specs, out_specs=out_specs, check_vma=False
    )
```

```python
import functools
import math

import jax
import jax.numpy as jnp
import numpy as np
from jax import lax
from jax.experimental import pallas as pl
from jax.experimental.pallas import tpu as pltpu
from jax.sharding import PartitionSpec as P

KR = 256
ROWS = 1024
COLS = 256
WIN = 8
BG = 16


def column_table(samples, parts):
    wide = COLS // parts + 2
    column = (np.arange(parts) * (wide - 2))[:, None] + np.arange(-1, wide - 1)[None, :]
    inside = (column >= 0) & (column < COLS)
    phase = ((np.arange(samples)[:, None, None] * column[None]) % samples) * (2.0 * math.pi / samples)
    cosine = np.where(inside, np.cos(phase), 0.0) / math.sqrt(samples)
    sine = np.where(inside, -np.sin(phase), 0.0) / math.sqrt(samples)
    upper = np.stack([cosine, sine], axis=2)
    lower = np.stack([-sine, cosine], axis=2)
    return jnp.asarray(np.concatenate([upper, lower], axis=0).astype(np.float32)).astype(jnp.bfloat16)


def row_table(rows):
    sample = jnp.arange(KR, dtype=jnp.int32)[:, None] - KR // 2
    phase = jnp.mod(rows[None, :] * sample, ROWS).astype(jnp.float32) * (2.0 * math.pi / ROWS)
    scale = jnp.where((rows >= 0) & (rows < ROWS), 1.0 / math.sqrt(KR), 0.0)[None, :]
    cosine = jnp.cos(phase) * scale
    sine = jnp.sin(phase) * scale
    upper = jnp.stack([cosine, sine], axis=1)
    lower = jnp.stack([-sine, cosine], axis=1)
    return jnp.concatenate([upper, lower], axis=0).astype(jnp.bfloat16)


def rotation(offsets, samples):
    angle = jnp.mod(offsets[:, None] * (samples[None, :] - KR // 2), ROWS).astype(jnp.float32) * (2.0 * math.pi / ROWS)
    return jnp.cos(angle), jnp.sin(angle)


def plain_body(spectra, offsets):
    own, depth = spectra.shape[:2]
    parts, strips = lax.axis_size("sub"), lax.axis_size("strip")
    wide = COLS // parts + 2
    high = ROWS // strips
    strip = lax.axis_index("strip")
    frames = own * parts
    table = column_table(spectra.shape[2] // 2, parts)
    cosine, sine = rotation(offsets, strip * depth + jnp.arange(depth, dtype=jnp.int32))
    mixed = jnp.einsum("skc,cdpn->dspnk", spectra, table, preferred_element_type=jnp.float32)
    real, imag = mixed[:, :, 0], mixed[:, :, 1]
    cosine, sine = cosine[None, :, None, :], sine[None, :, None, :]
    shifted = jnp.stack([real * cosine - imag * sine, real * sine + imag * cosine], axis=2).astype(jnp.bfloat16)
    held = lax.all_to_all(shifted, "sub", split_axis=0, concat_axis=0, tiled=True)
    held = held.reshape(frames, 2, wide, depth)
    whole = jnp.zeros((frames, 2, wide, strips, depth), jnp.bfloat16)
    for step in range(strips):
        part = held
        if step:
            part = lax.ppermute(held, "strip", [(i, (i + step) % strips) for i in range(strips)])
        source = jnp.mod(strip - step, strips)
        whole = lax.dynamic_update_slice(whole, part[:, :, :, None], (0, 0, 0, source, 0))
    wider = whole.reshape(frames, 2, wide, KR).astype(jnp.float32)
    summed = wider
    for lead in range(1, WIN):
        summed = summed + jnp.roll(wider, -lead, axis=0)
    rows = strip * high + jnp.arange(-1, high + 1, dtype=jnp.int32)
    product = jnp.einsum(
        "fpnk,pkqm->qnfm",
        summed.astype(jnp.bfloat16),
        row_table(rows).reshape(2, KR, 2, high + 2),
        preferred_element_type=jnp.float32,
    )
    log_power = jnp.log(1.0 + product[0] * product[0] + product[1] * product[1])
    total = log_power[:, :, :-2] + log_power[:, :, 1:-1] + log_power[:, :, 2:]
    filtered = (total[:-2] + total[1:-1] + total[2:]) / 9.0
    background = filtered
    for behind in range(1, BG):
        background = background + jnp.roll(filtered, behind, axis=1)
    return jnp.transpose(filtered - background / BG, (2, 0, 1))


LANES = 128
GROUP = 4
RADIX = 4
LAYERS = 4
MESH = pl.DeviceIdType.MESH


def column_planes(samples):
    phase = (np.arange(COLS)[:, None] * np.arange(samples // RADIX)[None, :] % samples) * (2.0 * math.pi / samples)
    cosine, sine = np.cos(phase) / math.sqrt(samples), -np.sin(phase) / math.sqrt(samples)
    planes = np.block([[[cosine, -sine]], [[sine, cosine]]])
    planes = planes.reshape(2, COLS // RADIX, RADIX, 2 * samples // RADIX).transpose(2, 0, 1, 3)
    planes = planes.reshape(RADIX, 2 * COLS // RADIX, 2 * samples // RADIX)
    return jnp.asarray(planes.astype(np.float32).astype(jnp.bfloat16))


def row_planes(high):
    row = np.concatenate([np.arange(high + LANES - 1), [-1]])
    used = (row <= high)[None, :]
    phase = (row[None, :] * (2 * np.arange(KR // 2)[:, None] + 1) % (2 * ROWS)) * (math.pi / ROWS)
    planes = np.concatenate([np.cos(phase) * used, -np.sin(phase) * used]) / math.sqrt(KR)
    return jnp.asarray(planes.astype(np.float32).astype(jnp.bfloat16))


def stages(upper):
    return [[2 * upper], [LAYERS - 1], [1 - upper, 2 - upper]]


def frame_weights(width, sources, rows):
    frames = 2 * sources
    weights = np.zeros((2, width, frames, rows), np.float32)
    target = np.arange(frames)

    def place(upper, at, column, frame):
        series = np.where(target == frame, 1.0, 0.0) - np.where((target - frame) % frames < BG, 1.0 / BG, 0.0)
        for near in range(max(column - 1, 0), min(column + 2, width)):
            weights[upper, near, :, at] = series

    for upper in range(2):
        at, edge_at = 0, frames * width
        for group in stages(upper):
            held = [layer * GROUP + index for layer in group for index in range(GROUP)]
            for lane in range(2):
                for source in held:
                    for spot in range(width):
                        place(upper, at, RADIX * (spot % (width // RADIX)) + spot // (width // RADIX), 2 * source + lane)
                        at += 1
            for lane in range(2):
                for source in held:
                    for side in range(2):
                        place(upper, edge_at, (-1, width)[side], 2 * source + lane)
                        edge_at += 1
    return jnp.asarray(weights.reshape(2, width * frames, rows).astype(jnp.bfloat16))


def product_of(a, b):
    return lax.dot_general(a, b, (((1,), (0,)), ((), ())), preferred_element_type=jnp.float32)


def product_t(a, b):
    return lax.dot_general(a, b, (((1,), (1,)), ((), ())), preferred_element_type=jnp.float32)


def kernel(
    parts, strips, offsets_hbm, spectra_hbm, columns_hbm, rows_hbm, weights_hbm, out_ref,
    offsets_ref, spectra, columns, rows, weights, mixed, ends, edge, main, held, lhs, boxed, level,
    load_sem, own_sem, send_sem, recv_sem, got_sem, entry_sem,
):
    me, strip = lax.axis_index("sub"), lax.axis_index("strip")
    width = COLS // parts
    depth = spectra.shape[1]
    samples = spectra.shape[2] // 2
    high = out_ref.shape[2]
    other = 1 - strip
    reach = LAYERS // 2
    layer, place = me // GROUP, lax.rem(me, GROUP)
    upper, within = layer // reach, lax.rem(layer, reach)

    def device_at(half, step, turn):
        return (half * reach + step) * GROUP + lax.rem(place + turn + GROUP, GROUP)

    def aside(step, shift, twist):
        row, core = lax.rem(place // 2 + shift, 2), lax.rem(place + twist, 2)
        return (upper * reach + lax.rem(within + step, reach)) * GROUP + 2 * row + core

    beside = [aside(0, 0, 1), aside(0, 1, 0), aside(0, 1, 1)]
    near = [aside(1, 0, 0), aside(1, 0, 1)]
    diagonal = [aside(1, 1, 0), aside(1, 1, 1)]
    close = beside + near + diagonal
    opening = layer == reach
    closing = layer == LAYERS - 1
    skipped = 2 * len(diagonal) * (layer // reach) * (1 - lax.rem(layer, reach))
    outward = [step for step in range(reach)]
    targets = [
        ((1 - upper) * reach + step) * GROUP + 2 * row + lax.rem(place + twist, 2)
        for step in outward for row in range(2) for twist in range(2)
    ]
    waits = [(step, turn) for step in range(2) for turn in range(GROUP)]
    origins = [
        ((1 - upper) * reach + (1 - upper) + (2 * upper - 1) * step) * GROUP + 2 * (turn % 2) + lax.rem(place + turn // 2, 2)
        for step, turn in waits
    ]

    def load(source, target, i):
        return pltpu.make_async_copy(source, target, load_sem.at[i])

    loads = [
        load(offsets_hbm, offsets_ref, 0),
        load(spectra_hbm, spectra, 1),
        load(columns_hbm, columns, 2),
        load(rows_hbm, rows, 3),
        load(weights_hbm.at[upper], weights, 4),
    ]
    piece = depth // 2
    loads[0].start()
    for own in range(2):
        for at in range(0, depth, piece):
            load(spectra_hbm.at[own, at : at + piece], spectra.at[own, at : at + piece], 1).start()
    loads[2].start()
    barrier = pltpu.get_barrier_semaphore()

    def announce(to, side):
        pl.semaphore_signal(barrier, inc=1, device_id=(to, side), device_id_type=MESH)

    for to in targets + beside + near:
        announce(to, strip)
    for to in [me] + beside + near:
        announce(to, other)

    @pl.when(jnp.logical_not(closing))
    def _():
        for to in diagonal:
            announce(to, strip)
            announce(to, other)

    edge[...] = jnp.zeros_like(edge)
    quarter = samples // RADIX
    loads[1].wait()
    for own in range(2):
        re = [spectra[own, :, p * quarter : (p + 1) * quarter].astype(jnp.float32) for p in range(RADIX)]
        im = [spectra[own, :, samples + p * quarter : samples + (p + 1) * quarter].astype(jnp.float32) for p in range(RADIX)]
        even_re, even_im, gap_re, gap_im = re[0] + re[2], im[0] + im[2], re[0] - re[2], im[0] - im[2]
        odd_re, odd_im, turn_re, turn_im = re[1] + re[3], im[1] + im[3], im[1] - im[3], re[3] - re[1]
        folded = [
            (even_re + odd_re, even_im + odd_im), (gap_re + turn_re, gap_im + turn_im),
            (even_re - odd_re, even_im - odd_im), (gap_re - turn_re, gap_im - turn_im),
        ]
        for residue, pair in enumerate(folded):
            for part, value in enumerate(pair):
                mixed[residue, own * depth : (own + 1) * depth, part * quarter : (part + 1) * quarter] = value.astype(jnp.bfloat16)
    loads[2].wait()
    loads[0].wait()
    lane = lax.broadcasted_iota(jnp.int32, (1, 2 * depth), 1)
    sample = strip * depth + jnp.where(lane < depth, lane, lane - depth) - KR // 2
    offset = jnp.where(lane < depth, offsets_ref[0], offsets_ref[1])
    angle = jnp.bitwise_and(offset * sample, ROWS - 1).astype(jnp.float32) * (2.0 * math.pi / ROWS)
    cosine, sine = jnp.cos(angle), jnp.sin(angle)
    for copy in loads[3:]:
        copy.start()
    rank = COLS // RADIX
    slots = width // RADIX
    back = lax.broadcasted_iota(jnp.int32, (rank, depth), 1)
    back = (1 - strip) * (depth - 1 - 2 * back) + back
    for residue in range(RADIX):
        both = product_t(columns[residue], mixed[residue])
        re, im = both[:rank], both[rank:]
        for part, value in ((0, re * cosine - im * sine), (1, re * sine + im * cosine)):
            for own in range(2):
                turned = jnp.take_along_axis(value[:, own * depth : (own + 1) * depth], back, axis=1, mode="promise_in_bounds")
                into = slice(part * depth, (part + 1) * depth)
                if residue == 0:
                    ends[2 * own + 1, :, into] = turned
                if residue == RADIX - 1:
                    ends[2 * own, :, into] = turned
                main[:, own * RADIX + residue, :, into] = (
                    turned.reshape(parts, slots, depth).astype(jnp.bfloat16)
                )
    for own in range(2):
        for d in range(parts):
            if d > 0:
                edge[d, 2 * own : 2 * own + 1] = ends[2 * own, d * slots - 1 : d * slots]
            if d < parts - 1:
                edge[d, 2 * own + 1 : 2 * own + 2] = ends[2 * own + 1, (d + 1) * slots : (d + 1) * slots + 1]
    main[:, 2 * RADIX] = edge[:, :4].astype(jnp.bfloat16)

    pl.semaphore_wait(barrier, parts + len(close) - skipped)

    def remote(source, h, to, side, sent, landed):
        return pltpu.make_async_remote_copy(
            src_ref=source, dst_ref=held.at[strip, h], send_sem=sent, recv_sem=landed,
            device_id=(to, side), device_id_type=MESH,
        )

    def send(to):
        return remote(main.at[to], me, to, strip, send_sem.at[0], recv_sem.at[parts // 2])

    def send_far(to):
        return remote(main.at[to], me, to, strip, send_sem.at[0], recv_sem.at[lax.rem(me, parts // 2)])

    def cross(to):
        return remote(main.at[to], me, to, other, send_sem.at[1], got_sem.at[0])

    def forward(source, group):
        return remote(held.at[strip, source], source, me, other, send_sem.at[1], got_sem.at[1 + group])

    def far_arrival(source):
        sem = recv_sem.at[lax.rem(source, parts // 2)]
        return pltpu.make_async_copy(main.at[source], held.at[strip, source], sem)

    def together(h, number, sem):
        return pltpu.make_async_copy(main.at[pl.ds(0, number)], held.at[h, pl.ds(0, number)], sem)

    for index, to in enumerate(targets):
        send_far(to).start()
        if index < len(close) - 1:
            cross(([me] + beside + near)[index]).start()
    for to in beside + near:
        send(to).start()

    def send_diagonal():
        for to in diagonal:
            send(to).start()
            cross(to).start()

    pl.when(jnp.logical_not(opening))(send_diagonal)

    @pl.when(closing)
    def _():
        for to in diagonal:
            pl.semaphore_signal(entry_sem, inc=1, device_id=(to, strip), device_id_type=MESH)
            pl.semaphore_signal(entry_sem, inc=1, device_id=(to, other), device_id_type=MESH)

    kept = pltpu.make_async_copy(main.at[me], held.at[strip, me], own_sem.at[0])
    kept.start()

    @pl.when(opening)
    def _():
        pl.semaphore_wait(entry_sem, 2 * len(diagonal))
        send_diagonal()


    alternate = 1.0 - 2.0 * lax.rem(lax.broadcasted_iota(jnp.int32, (1, 1, 2 * depth), 2), 2).astype(jnp.float32)

    def sign_of(h):
        return 1.0 - strip * (1.0 + (1 - 2 * h) * alternate)

    row_at = lax.broadcasted_iota(jnp.int32, (GROUP, 8, 2 * depth), 1)

    def window(h, first, count):
        block = []
        for step in range(count + 1):
            at = lax.rem(first + step, LAYERS) * GROUP
            block.append(held[h, pl.ds(at, GROUP)].astype(jnp.float32) * sign_of(h)[None])
        whole = jnp.concatenate(block, axis=0)
        number = count * GROUP
        body = whole[:, : 2 * RADIX].reshape(number + GROUP, 2 * width, 2 * depth)
        near = whole[:, 2 * RADIX]
        near = jnp.concatenate([near, jnp.zeros_like(near)], axis=1)
        near_second = jnp.concatenate([pltpu.roll(near[i], 6, 0)[None] for i in range(number + GROUP)], axis=0)
        results = []
        for one, two in ((body[:, :width], body[:, width:]), (near, near_second)):
            pair = one + two
            double = pair[:-1] + pair[1:]
            quad = double[:number] + double[2 : number + 2]
            results.append((quad, quad - one[:number] + one[WIN // 2 : number + WIN // 2]))
        packed = []
        for frame in results[1]:
            for group in range(count):
                masked = jnp.where(row_at < 2, frame[GROUP * group : GROUP * (group + 1)], 0.0)
                total = masked[0]
                for j in range(1, GROUP):
                    total = total + pltpu.roll(masked[j], 2 * j, 0)
                packed.append(total)
        flat = [frame.reshape(number * width, 2 * depth) for frame in results[0]]
        return jnp.concatenate(flat + packed, axis=0)

    tail = lax.broadcasted_iota(jnp.int32, (1, high + LANES), 1)
    outside = ((tail == high) & (strip == strips - 1)) | ((tail == high + LANES - 1) & (strip == 0))
    inside = jnp.where(outside, 0.0, 1.0)

    facing = (2 * strip - 1).astype(jnp.float32)

    def image(mine, theirs):
        total = mine + theirs
        gap = (mine - theirs) * facing
        size = total.shape[0]
        lhs[:size, :depth] = total[:, :depth].astype(jnp.bfloat16)
        lhs[:size, depth:] = gap[:, depth:].astype(jnp.bfloat16)
        lhs[size : 2 * size, :depth] = total[:, depth:].astype(jnp.bfloat16)
        lhs[size : 2 * size, depth:] = (-gap[:, :depth]).astype(jnp.bfloat16)
        step = size // 2
        pieces = []
        for at in range(0, size, step):
            re = product_of(lhs[at : at + step], rows[...])
            im = product_of(lhs[size + at : size + at + step], rows[...])
            power = jnp.log(1.0 + re * re + im * im) * inside
            pieces.append((power + pltpu.roll(power, 1, 1) + pltpu.roll(power, high + LANES - 1, 1))[:, :high])
        return pieces

    batch = GROUP * width
    for index, source in enumerate(origins):
        far_arrival(source).wait()
        forward(source, waits[index][0]).start()
    together(strip, len(close), recv_sem.at[parts // 2]).wait()
    kept.wait()
    together(other, parts // 2, got_sem.at[0]).wait()
    loads[3].wait()
    pieces = image(window(strip, 2 * upper, 1), window(other, 2 * upper, 1))
    size = 2 * batch + 2 * 8
    for i, piece in enumerate(pieces):
        boxed[0, i * (size // 2) : (i + 1) * (size // 2)] = piece
    together(other, GROUP, got_sem.at[1]).wait()
    pieces = image(window(strip, LAYERS - 1, 1), window(other, LAYERS - 1, 1))
    for i, piece in enumerate(pieces):
        boxed[1, i * (size // 2) : (i + 1) * (size // 2)] = piece
    early = boxed[:, : 2 * batch].reshape(2, 2 * GROUP, width, high)
    mean = jnp.sum(jnp.sum(early, axis=0), axis=0) * (1.0 / (4 * GROUP))
    for i in range(2):
        level[2 * batch * i : 2 * batch * (i + 1)] = (early[i] - mean[None]).reshape(2 * batch, high).astype(jnp.bfloat16)
    early_near = boxed[:, 2 * batch : size].reshape(4, 8, high)
    near_mean = jnp.sum(early_near, axis=0) * (1.0 / (4 * GROUP))
    near_mean = near_mean + pltpu.roll(near_mean, 4, 0)
    near_mean = near_mean + pltpu.roll(near_mean, 2, 0)
    top = 2 * parts * width
    level[top : top + 32] = (early_near - near_mean[None]).reshape(32, high).astype(jnp.bfloat16)
    level[top + 64 :] = jnp.zeros((level.shape[0] - top - 64, high), jnp.bfloat16)

    loads[4].wait()
    frames = 2 * parts
    step = 16
    for c in range(0, width, step):
        piece = product_of(weights[c * frames : (c + step) * frames, : 4 * batch], level[: 4 * batch])
        out_ref[c : c + step] = piece.reshape(step, frames, high)
    mine = window(strip, 1 - upper, 2)
    together(other, GROUP, got_sem.at[2]).wait()
    pieces = image(mine, window(other, 1 - upper, 2))
    late = jnp.concatenate(pieces, axis=0)
    block = late[: 4 * batch].reshape(4 * GROUP, width, high)
    level[4 * batch : 8 * batch] = (block - mean[None]).reshape(4 * batch, high).astype(jnp.bfloat16)
    late_near = late[4 * batch :].reshape(4, 8, high)
    level[top + 32 : top + 64] = (late_near - near_mean[None]).reshape(32, high).astype(jnp.bfloat16)
    for c in range(0, width, step):
        piece = product_of(weights[c * frames : (c + step) * frames, 4 * batch : 8 * batch], level[4 * batch : 8 * batch])
        piece = out_ref[c : c + step] + piece.reshape(step, frames, high)
        for edge_column in (0, width - 1):
            if c <= edge_column < c + step:
                extra = product_of(weights[edge_column * frames : (edge_column + 1) * frames, 8 * batch :], level[8 * batch :])
                row = edge_column - c
                parts_of = [piece[:row], piece[row : row + 1] + extra[None], piece[row + 1 :]]
                piece = jnp.concatenate([part for part in parts_of if part.shape[0]], axis=0)
        out_ref[c : c + step] = piece * (1.0 / 9.0)
    together(strip, parts - 1, send_sem.at[0]).wait()
    together(strip, parts, send_sem.at[1]).wait()


def kernel_body(spectra, offsets):
    parts, strips = lax.axis_size("sub"), lax.axis_size("strip")
    own, depth, both = spectra.shape
    width, high = COLS // parts, ROWS // strips
    frames = own * parts
    total_rows = frames * (width + 2)
    padded = -(-total_rows // LANES) * LANES
    bf16, f32 = jnp.bfloat16, jnp.float32
    operands = (offsets, spectra, column_planes(both // 2), row_planes(high), frame_weights(width, parts, padded))
    shapes = [operand.shape for operand in operands[1:4]] + [operands[4].shape[1:]]
    half = 2 * GROUP * width + 2 * 8
    out = pl.pallas_call(
        functools.partial(kernel, parts, strips),
        out_shape=jax.ShapeDtypeStruct((width, frames, high), f32),
        in_specs=[pl.BlockSpec(memory_space=pltpu.HBM)] * 5,
        out_specs=pl.BlockSpec(memory_space=pltpu.VMEM),
        scratch_shapes=[pltpu.SMEM(offsets.shape, offsets.dtype)]
        + [pltpu.VMEM(shape, bf16) for shape in shapes]
        + [
            pltpu.VMEM((RADIX, 2 * depth, both // RADIX), bf16),
            pltpu.VMEM((4, COLS // RADIX, 2 * depth), f32),
            pltpu.VMEM((parts, 8, 2 * depth), f32),
            pltpu.VMEM((parts, 2 * RADIX + 1, width // RADIX, 2 * depth), bf16),
            pltpu.VMEM((strips, parts, 2 * RADIX + 1, width // RADIX, 2 * depth), bf16),
            pltpu.VMEM((4 * half, KR), bf16),
            pltpu.VMEM((2, half, high), f32),
            pltpu.VMEM((padded, high), bf16),
            pltpu.SemaphoreType.DMA((5,)),
            pltpu.SemaphoreType.DMA((1,)),
            pltpu.SemaphoreType.DMA((2,)),
            pltpu.SemaphoreType.DMA((parts // 2 + 1,)),
            pltpu.SemaphoreType.DMA((3,)),
            pltpu.SemaphoreType.REGULAR,
        ],
        compiler_params=pltpu.CompilerParams(collective_id=0, has_side_effects=True, vmem_limit_bytes=48 << 20),
        name="sar",
    )(*(pltpu.with_memory_space_constraint(operand, pltpu.HBM) for operand in operands))
    return jnp.transpose(out, (2, 0, 1))


def fits(mesh):
    parts, strips = mesh.shape["sub"], mesh.shape["strip"]
    return strips == 2 and KR // strips == LANES and COLS % parts == 0 and COLS // parts == 16 and parts == LAYERS * GROUP


def body(mesh, spectra, offsets):
    if fits(mesh) and spectra.shape[0] == 2:
        return kernel_body(spectra, offsets)
    return plain_body(spectra, offsets)


def solution(mesh):
    in_specs = (P("sub", "strip", None), P("sub"))
    out_specs = P("strip", "sub", None)
    return jax.shard_map(
        functools.partial(body, mesh), mesh=mesh, in_specs=in_specs, out_specs=out_specs, check_vma=False
    )
```

```python
import functools
import math

import jax
import jax.numpy as jnp
import numpy as np
from jax import lax
from jax.experimental import pallas as pl
from jax.experimental.pallas import tpu as pltpu
from jax.sharding import PartitionSpec as P

KR = 256
ROWS = 1024
COLS = 256
WIN = 8
BG = 16


def column_table(samples, parts):
    wide = COLS // parts + 2
    column = (np.arange(parts) * (wide - 2))[:, None] + np.arange(-1, wide - 1)[None, :]
    inside = (column >= 0) & (column < COLS)
    phase = ((np.arange(samples)[:, None, None] * column[None]) % samples) * (2.0 * math.pi / samples)
    cosine = np.where(inside, np.cos(phase), 0.0) / math.sqrt(samples)
    sine = np.where(inside, -np.sin(phase), 0.0) / math.sqrt(samples)
    upper = np.stack([cosine, sine], axis=2)
    lower = np.stack([-sine, cosine], axis=2)
    return jnp.asarray(np.concatenate([upper, lower], axis=0).astype(np.float32)).astype(jnp.bfloat16)


def row_table(rows):
    sample = jnp.arange(KR, dtype=jnp.int32)[:, None] - KR // 2
    phase = jnp.mod(rows[None, :] * sample, ROWS).astype(jnp.float32) * (2.0 * math.pi / ROWS)
    scale = jnp.where((rows >= 0) & (rows < ROWS), 1.0 / math.sqrt(KR), 0.0)[None, :]
    cosine = jnp.cos(phase) * scale
    sine = jnp.sin(phase) * scale
    upper = jnp.stack([cosine, sine], axis=1)
    lower = jnp.stack([-sine, cosine], axis=1)
    return jnp.concatenate([upper, lower], axis=0).astype(jnp.bfloat16)


def rotation(offsets, samples):
    angle = jnp.mod(offsets[:, None] * (samples[None, :] - KR // 2), ROWS).astype(jnp.float32) * (2.0 * math.pi / ROWS)
    return jnp.cos(angle), jnp.sin(angle)


def plain_body(spectra, offsets):
    own, depth = spectra.shape[:2]
    parts, strips = lax.axis_size("sub"), lax.axis_size("strip")
    wide = COLS // parts + 2
    high = ROWS // strips
    strip = lax.axis_index("strip")
    frames = own * parts
    table = column_table(spectra.shape[2] // 2, parts)
    cosine, sine = rotation(offsets, strip * depth + jnp.arange(depth, dtype=jnp.int32))
    mixed = jnp.einsum("skc,cdpn->dspnk", spectra, table, preferred_element_type=jnp.float32)
    real, imag = mixed[:, :, 0], mixed[:, :, 1]
    cosine, sine = cosine[None, :, None, :], sine[None, :, None, :]
    shifted = jnp.stack([real * cosine - imag * sine, real * sine + imag * cosine], axis=2).astype(jnp.bfloat16)
    held = lax.all_to_all(shifted, "sub", split_axis=0, concat_axis=0, tiled=True)
    held = held.reshape(frames, 2, wide, depth)
    whole = jnp.zeros((frames, 2, wide, strips, depth), jnp.bfloat16)
    for step in range(strips):
        part = held
        if step:
            part = lax.ppermute(held, "strip", [(i, (i + step) % strips) for i in range(strips)])
        source = jnp.mod(strip - step, strips)
        whole = lax.dynamic_update_slice(whole, part[:, :, :, None], (0, 0, 0, source, 0))
    wider = whole.reshape(frames, 2, wide, KR).astype(jnp.float32)
    summed = wider
    for lead in range(1, WIN):
        summed = summed + jnp.roll(wider, -lead, axis=0)
    rows = strip * high + jnp.arange(-1, high + 1, dtype=jnp.int32)
    product = jnp.einsum(
        "fpnk,pkqm->qnfm",
        summed.astype(jnp.bfloat16),
        row_table(rows).reshape(2, KR, 2, high + 2),
        preferred_element_type=jnp.float32,
    )
    log_power = jnp.log(1.0 + product[0] * product[0] + product[1] * product[1])
    total = log_power[:, :, :-2] + log_power[:, :, 1:-1] + log_power[:, :, 2:]
    filtered = (total[:-2] + total[1:-1] + total[2:]) / 9.0
    background = filtered
    for behind in range(1, BG):
        background = background + jnp.roll(filtered, behind, axis=1)
    return jnp.transpose(filtered - background / BG, (2, 0, 1))


LANES = 128
GROUP = 4
RADIX = 4
LAYERS = 4
MESH = pl.DeviceIdType.MESH


def column_planes(samples):
    phase = (np.arange(COLS)[:, None] * np.arange(samples // RADIX)[None, :] % samples) * (2.0 * math.pi / samples)
    cosine, sine = np.cos(phase) / math.sqrt(samples), -np.sin(phase) / math.sqrt(samples)
    planes = np.block([[[cosine, -sine]], [[sine, cosine]]])
    planes = planes.reshape(2, COLS // RADIX, RADIX, 2 * samples // RADIX).transpose(2, 0, 1, 3)
    planes = planes.reshape(RADIX, 2 * COLS // RADIX, 2 * samples // RADIX)
    return jnp.asarray(planes.astype(np.float32).astype(jnp.bfloat16))


def row_planes(high):
    row = np.concatenate([np.arange(high + LANES - 1), [-1]])
    used = (row <= high)[None, :]
    phase = (row[None, :] * (2 * np.arange(KR // 2)[:, None] + 1) % (2 * ROWS)) * (math.pi / ROWS)
    planes = np.concatenate([np.cos(phase) * used, -np.sin(phase) * used]) / math.sqrt(KR)
    return jnp.asarray(planes.astype(np.float32).astype(jnp.bfloat16))


def stages(upper):
    return [[2 * upper], [LAYERS - 1], [1 - upper, 2 - upper]]


def frame_weights(width, sources, rows):
    frames = 2 * sources
    weights = np.zeros((2, width, frames, rows), np.float32)
    target = np.arange(frames)

    def place(upper, at, column, frame):
        series = np.where(target == frame, 1.0, 0.0) - np.where((target - frame) % frames < BG, 1.0 / BG, 0.0)
        for near in range(max(column - 1, 0), min(column + 2, width)):
            weights[upper, near, :, at] = series

    for upper in range(2):
        at, edge_at = 0, frames * width
        for group in stages(upper):
            held = [layer * GROUP + index for layer in group for index in range(GROUP)]
            for lane in range(2):
                for source in held:
                    for spot in range(width):
                        place(upper, at, RADIX * (spot % (width // RADIX)) + spot // (width // RADIX), 2 * source + lane)
                        at += 1
            for lane in range(2):
                for source in held:
                    for side in range(2):
                        place(upper, edge_at, (-1, width)[side], 2 * source + lane)
                        edge_at += 1
    return jnp.asarray(weights.reshape(2, width * frames, rows).astype(jnp.bfloat16))


def product_of(a, b):
    return lax.dot_general(a, b, (((1,), (0,)), ((), ())), preferred_element_type=jnp.float32)


def product_t(a, b):
    return lax.dot_general(a, b, (((1,), (1,)), ((), ())), preferred_element_type=jnp.float32)


def kernel(
    parts, strips, offsets_hbm, spectra_hbm, columns_hbm, rows_hbm, weights_hbm, out_ref,
    offsets_ref, spectra, columns, rows, weights, mixed, ends, edge, main, held, lhs, boxed, level,
    load_sem, own_sem, send_sem, recv_sem, got_sem, entry_sem,
):
    me, strip = lax.axis_index("sub"), lax.axis_index("strip")
    width = COLS // parts
    depth = spectra.shape[1]
    samples = spectra.shape[2] // 2
    high = out_ref.shape[2]
    other = 1 - strip
    reach = LAYERS // 2
    layer, place = me // GROUP, lax.rem(me, GROUP)
    upper, within = layer // reach, lax.rem(layer, reach)

    def device_at(half, step, turn):
        return (half * reach + step) * GROUP + lax.rem(place + turn + GROUP, GROUP)

    def aside(step, shift, twist):
        row, core = lax.rem(place // 2 + shift, 2), lax.rem(place + twist, 2)
        return (upper * reach + lax.rem(within + step, reach)) * GROUP + 2 * row + core

    beside = [aside(0, 0, 1), aside(0, 1, 0), aside(0, 1, 1)]
    near = [aside(1, 0, 0), aside(1, 0, 1)]
    diagonal = [aside(1, 1, 0), aside(1, 1, 1)]
    close = beside + near + diagonal
    opening = layer == reach
    closing = layer == LAYERS - 1
    skipped = 2 * len(diagonal) * (layer // reach) * (1 - lax.rem(layer, reach))
    outward = [step for step in range(reach)]
    targets = [
        ((1 - upper) * reach + step) * GROUP + 2 * row + lax.rem(place + twist, 2)
        for step in outward for row in range(2) for twist in range(2)
    ]
    waits = [(step, turn) for step in range(2) for turn in range(GROUP)]
    origins = [
        ((1 - upper) * reach + (1 - upper) + (2 * upper - 1) * step) * GROUP + 2 * (turn % 2) + lax.rem(place + turn // 2, 2)
        for step, turn in waits
    ]

    def load(source, target, i):
        return pltpu.make_async_copy(source, target, load_sem.at[i])

    loads = [
        load(offsets_hbm, offsets_ref, 0),
        load(spectra_hbm, spectra, 1),
        load(columns_hbm, columns, 2),
        load(rows_hbm, rows, 3),
        load(weights_hbm.at[upper], weights, 4),
    ]
    piece = depth // 2
    loads[0].start()
    for own in range(2):
        for at in range(0, depth, piece):
            load(spectra_hbm.at[own, at : at + piece], spectra.at[own, at : at + piece], 1).start()
    loads[2].start()
    barrier = pltpu.get_barrier_semaphore()

    def announce(to, side):
        pl.semaphore_signal(barrier, inc=1, device_id=(to, side), device_id_type=MESH)

    for to in targets + beside + near:
        announce(to, strip)
    for to in [me] + beside + near:
        announce(to, other)

    @pl.when(jnp.logical_not(closing))
    def _():
        for to in diagonal:
            announce(to, strip)
            announce(to, other)

    edge[...] = jnp.zeros_like(edge)
    quarter = samples // RADIX
    loads[1].wait()
    for own in range(2):
        re = [spectra[own, :, p * quarter : (p + 1) * quarter].astype(jnp.float32) for p in range(RADIX)]
        im = [spectra[own, :, samples + p * quarter : samples + (p + 1) * quarter].astype(jnp.float32) for p in range(RADIX)]
        even_re, even_im, gap_re, gap_im = re[0] + re[2], im[0] + im[2], re[0] - re[2], im[0] - im[2]
        odd_re, odd_im, turn_re, turn_im = re[1] + re[3], im[1] + im[3], im[1] - im[3], re[3] - re[1]
        folded = [
            (even_re + odd_re, even_im + odd_im), (gap_re + turn_re, gap_im + turn_im),
            (even_re - odd_re, even_im - odd_im), (gap_re - turn_re, gap_im - turn_im),
        ]
        for residue, pair in enumerate(folded):
            for part, value in enumerate(pair):
                mixed[residue, own * depth : (own + 1) * depth, part * quarter : (part + 1) * quarter] = value.astype(jnp.bfloat16)
    loads[2].wait()
    loads[0].wait()
    lane = lax.broadcasted_iota(jnp.int32, (1, 2 * depth), 1)
    sample = strip * depth + jnp.where(lane < depth, lane, lane - depth) - KR // 2
    offset = jnp.where(lane < depth, offsets_ref[0], offsets_ref[1])
    angle = jnp.bitwise_and(offset * sample, ROWS - 1).astype(jnp.float32) * (2.0 * math.pi / ROWS)
    cosine, sine = jnp.cos(angle), jnp.sin(angle)
    for copy in loads[3:]:
        copy.start()
    rank = COLS // RADIX
    slots = width // RADIX
    back = lax.broadcasted_iota(jnp.int32, (rank, depth), 1)
    back = (1 - strip) * (depth - 1 - 2 * back) + back
    for residue in range(RADIX):
        both = product_t(columns[residue], mixed[residue])
        re, im = both[:rank], both[rank:]
        for part, value in ((0, re * cosine - im * sine), (1, re * sine + im * cosine)):
            for own in range(2):
                turned = jnp.take_along_axis(value[:, own * depth : (own + 1) * depth], back, axis=1, mode="promise_in_bounds")
                into = slice(part * depth, (part + 1) * depth)
                if residue == 0:
                    ends[2 * own + 1, :, into] = turned
                if residue == RADIX - 1:
                    ends[2 * own, :, into] = turned
                main[:, own * RADIX + residue, :, into] = (
                    turned.reshape(parts, slots, depth).astype(jnp.bfloat16)
                )
    for own in range(2):
        for d in range(parts):
            if d > 0:
                edge[d, 2 * own : 2 * own + 1] = ends[2 * own, d * slots - 1 : d * slots]
            if d < parts - 1:
                edge[d, 2 * own + 1 : 2 * own + 2] = ends[2 * own + 1, (d + 1) * slots : (d + 1) * slots + 1]
    main[:, 2 * RADIX] = edge[:, :4].astype(jnp.bfloat16)

    pl.semaphore_wait(barrier, parts + len(close) - skipped)

    def remote(source, h, to, side, sent, landed):
        return pltpu.make_async_remote_copy(
            src_ref=source, dst_ref=held.at[strip, h], send_sem=sent, recv_sem=landed,
            device_id=(to, side), device_id_type=MESH,
        )

    def send(to):
        return remote(main.at[to], me, to, strip, send_sem.at[0], recv_sem.at[2 * reach])

    def send_far(to):
        return remote(main.at[to], me, to, strip, send_sem.at[0], recv_sem.at[2 * within + lax.rem(place, 2)])

    def cross(to):
        return remote(main.at[to], me, to, other, send_sem.at[1], got_sem.at[0])

    def forward(source, group):
        return remote(held.at[strip, source], source, me, other, send_sem.at[1], got_sem.at[1 + group])

    def together(h, number, sem):
        return pltpu.make_async_copy(main.at[pl.ds(0, number)], held.at[h, pl.ds(0, number)], sem)

    for index, to in enumerate(targets):
        send_far(to).start()
        if index < len(close) - 1:
            cross(([me] + beside + near)[index]).start()
    for to in beside + near:
        send(to).start()

    def send_diagonal():
        for to in diagonal:
            send(to).start()
            cross(to).start()

    pl.when(jnp.logical_not(opening))(send_diagonal)

    @pl.when(closing)
    def _():
        for to in diagonal:
            pl.semaphore_signal(entry_sem, inc=1, device_id=(to, strip), device_id_type=MESH)
            pl.semaphore_signal(entry_sem, inc=1, device_id=(to, other), device_id_type=MESH)

    kept = pltpu.make_async_copy(main.at[me], held.at[strip, me], own_sem.at[0])
    kept.start()

    @pl.when(opening)
    def _():
        pl.semaphore_wait(entry_sem, 2 * len(diagonal))
        send_diagonal()


    alternate = 1.0 - 2.0 * lax.rem(lax.broadcasted_iota(jnp.int32, (1, 1, 2 * depth), 2), 2).astype(jnp.float32)

    def sign_of(h):
        return 1.0 - strip * (1.0 + (1 - 2 * h) * alternate)

    row_at = lax.broadcasted_iota(jnp.int32, (GROUP, 8, 2 * depth), 1)

    def window(h, first, count):
        block = []
        for step in range(count + 1):
            at = lax.rem(first + step, LAYERS) * GROUP
            block.append(held[h, pl.ds(at, GROUP)].astype(jnp.float32) * sign_of(h)[None])
        whole = jnp.concatenate(block, axis=0)
        number = count * GROUP
        body = whole[:, : 2 * RADIX].reshape(number + GROUP, 2 * width, 2 * depth)
        near = whole[:, 2 * RADIX]
        near = jnp.concatenate([near, jnp.zeros_like(near)], axis=1)
        near_second = jnp.concatenate([pltpu.roll(near[i], 6, 0)[None] for i in range(number + GROUP)], axis=0)
        results = []
        for one, two in ((body[:, :width], body[:, width:]), (near, near_second)):
            pair = one + two
            double = pair[:-1] + pair[1:]
            quad = double[:number] + double[2 : number + 2]
            results.append((quad, quad - one[:number] + one[WIN // 2 : number + WIN // 2]))
        packed = []
        for frame in results[1]:
            for group in range(count):
                masked = jnp.where(row_at < 2, frame[GROUP * group : GROUP * (group + 1)], 0.0)
                total = masked[0]
                for j in range(1, GROUP):
                    total = total + pltpu.roll(masked[j], 2 * j, 0)
                packed.append(total)
        flat = [frame.reshape(number * width, 2 * depth) for frame in results[0]]
        return jnp.concatenate(flat + packed, axis=0)

    tail = lax.broadcasted_iota(jnp.int32, (1, high + LANES), 1)
    outside = ((tail == high) & (strip == strips - 1)) | ((tail == high + LANES - 1) & (strip == 0))
    inside = jnp.where(outside, 0.0, 1.0)

    facing = (2 * strip - 1).astype(jnp.float32)

    def image(mine, theirs):
        total = mine + theirs
        gap = (mine - theirs) * facing
        size = total.shape[0]
        lhs[:size, :depth] = total[:, :depth].astype(jnp.bfloat16)
        lhs[:size, depth:] = gap[:, depth:].astype(jnp.bfloat16)
        lhs[size : 2 * size, :depth] = total[:, depth:].astype(jnp.bfloat16)
        lhs[size : 2 * size, depth:] = (-gap[:, :depth]).astype(jnp.bfloat16)
        step = size // 2
        pieces = []
        for at in range(0, size, step):
            re = product_of(lhs[at : at + step], rows[...])
            im = product_of(lhs[size + at : size + at + step], rows[...])
            power = jnp.log(1.0 + re * re + im * im) * inside
            pieces.append((power + pltpu.roll(power, 1, 1) + pltpu.roll(power, high + LANES - 1, 1))[:, :high])
        return pieces

    batch = GROUP * width
    for index in range(0, len(origins), 2):
        source = origins[index]
        sem = recv_sem.at[2 * lax.rem(source // GROUP, reach) + lax.rem(source, 2)]
        together(strip, 2, sem).wait()
        for pair in origins[index : index + 2]:
            forward(pair, index // GROUP).start()
    together(strip, len(close), recv_sem.at[2 * reach]).wait()
    kept.wait()
    together(other, parts // 2, got_sem.at[0]).wait()
    loads[3].wait()
    pieces = image(window(strip, 2 * upper, 1), window(other, 2 * upper, 1))
    size = 2 * batch + 2 * 8
    for i, piece in enumerate(pieces):
        boxed[0, i * (size // 2) : (i + 1) * (size // 2)] = piece
    together(other, GROUP, got_sem.at[1]).wait()
    pieces = image(window(strip, LAYERS - 1, 1), window(other, LAYERS - 1, 1))
    for i, piece in enumerate(pieces):
        boxed[1, i * (size // 2) : (i + 1) * (size // 2)] = piece
    early = boxed[:, : 2 * batch].reshape(2, 2 * GROUP, width, high)
    mean = jnp.sum(jnp.sum(early, axis=0), axis=0) * (1.0 / (4 * GROUP))
    for i in range(2):
        level[2 * batch * i : 2 * batch * (i + 1)] = (early[i] - mean[None]).reshape(2 * batch, high).astype(jnp.bfloat16)
    early_near = boxed[:, 2 * batch : size].reshape(4, 8, high)
    near_mean = jnp.sum(early_near, axis=0) * (1.0 / (4 * GROUP))
    near_mean = near_mean + pltpu.roll(near_mean, 4, 0)
    near_mean = near_mean + pltpu.roll(near_mean, 2, 0)
    top = 2 * parts * width
    level[top : top + 32] = (early_near - near_mean[None]).reshape(32, high).astype(jnp.bfloat16)
    level[top + 64 :] = jnp.zeros((level.shape[0] - top - 64, high), jnp.bfloat16)

    loads[4].wait()
    frames = 2 * parts
    step = 16
    for c in range(0, width, step):
        piece = product_of(weights[c * frames : (c + step) * frames, : 4 * batch], level[: 4 * batch])
        out_ref[c : c + step] = piece.reshape(step, frames, high)
    mine = window(strip, 1 - upper, 2)
    together(other, GROUP, got_sem.at[2]).wait()
    pieces = image(mine, window(other, 1 - upper, 2))
    late = jnp.concatenate(pieces, axis=0)
    block = late[: 4 * batch].reshape(4 * GROUP, width, high)
    level[4 * batch : 8 * batch] = (block - mean[None]).reshape(4 * batch, high).astype(jnp.bfloat16)
    late_near = late[4 * batch :].reshape(4, 8, high)
    level[top + 32 : top + 64] = (late_near - near_mean[None]).reshape(32, high).astype(jnp.bfloat16)
    for c in range(0, width, step):
        piece = product_of(weights[c * frames : (c + step) * frames, 4 * batch : 8 * batch], level[4 * batch : 8 * batch])
        piece = out_ref[c : c + step] + piece.reshape(step, frames, high)
        for edge_column in (0, width - 1):
            if c <= edge_column < c + step:
                extra = product_of(weights[edge_column * frames : (edge_column + 1) * frames, 8 * batch :], level[8 * batch :])
                row = edge_column - c
                parts_of = [piece[:row], piece[row : row + 1] + extra[None], piece[row + 1 :]]
                piece = jnp.concatenate([part for part in parts_of if part.shape[0]], axis=0)
        out_ref[c : c + step] = piece * (1.0 / 9.0)
    together(strip, parts - 1, send_sem.at[0]).wait()
    together(strip, parts, send_sem.at[1]).wait()


def kernel_body(spectra, offsets):
    parts, strips = lax.axis_size("sub"), lax.axis_size("strip")
    own, depth, both = spectra.shape
    width, high = COLS // parts, ROWS // strips
    frames = own * parts
    total_rows = frames * (width + 2)
    padded = -(-total_rows // LANES) * LANES
    bf16, f32 = jnp.bfloat16, jnp.float32
    operands = (offsets, spectra, column_planes(both // 2), row_planes(high), frame_weights(width, parts, padded))
    shapes = [operand.shape for operand in operands[1:4]] + [operands[4].shape[1:]]
    half = 2 * GROUP * width + 2 * 8
    out = pl.pallas_call(
        functools.partial(kernel, parts, strips),
        out_shape=jax.ShapeDtypeStruct((width, frames, high), f32),
        in_specs=[pl.BlockSpec(memory_space=pltpu.HBM)] * 5,
        out_specs=pl.BlockSpec(memory_space=pltpu.VMEM),
        scratch_shapes=[pltpu.SMEM(offsets.shape, offsets.dtype)]
        + [pltpu.VMEM(shape, bf16) for shape in shapes]
        + [
            pltpu.VMEM((RADIX, 2 * depth, both // RADIX), bf16),
            pltpu.VMEM((4, COLS // RADIX, 2 * depth), f32),
            pltpu.VMEM((parts, 8, 2 * depth), f32),
            pltpu.VMEM((parts, 2 * RADIX + 1, width // RADIX, 2 * depth), bf16),
            pltpu.VMEM((strips, parts, 2 * RADIX + 1, width // RADIX, 2 * depth), bf16),
            pltpu.VMEM((4 * half, KR), bf16),
            pltpu.VMEM((2, half, high), f32),
            pltpu.VMEM((padded, high), bf16),
            pltpu.SemaphoreType.DMA((5,)),
            pltpu.SemaphoreType.DMA((1,)),
            pltpu.SemaphoreType.DMA((2,)),
            pltpu.SemaphoreType.DMA((5,)),
            pltpu.SemaphoreType.DMA((3,)),
            pltpu.SemaphoreType.REGULAR,
        ],
        compiler_params=pltpu.CompilerParams(collective_id=0, has_side_effects=True, vmem_limit_bytes=48 << 20),
        name="sar",
    )(*(pltpu.with_memory_space_constraint(operand, pltpu.HBM) for operand in operands))
    return jnp.transpose(out, (2, 0, 1))


def fits(mesh):
    parts, strips = mesh.shape["sub"], mesh.shape["strip"]
    return strips == 2 and KR // strips == LANES and COLS % parts == 0 and COLS // parts == 16 and parts == LAYERS * GROUP


def body(mesh, spectra, offsets):
    if fits(mesh) and spectra.shape[0] == 2:
        return kernel_body(spectra, offsets)
    return plain_body(spectra, offsets)


def solution(mesh):
    in_specs = (P("sub", "strip", None), P("sub"))
    out_specs = P("strip", "sub", None)
    return jax.shard_map(
        functools.partial(body, mesh), mesh=mesh, in_specs=in_specs, out_specs=out_specs, check_vma=False
    )
```
